32 devices in a mesh: dp: 8 (over z, y), tensor: 4 (over x, core).
Axes of the slice: x: 2, y: 2, z: 4, core: 2. Of those that a mesh axis runs over, the one named last changes fastest.
Arguments:
- tokens: bfloat16 [8192, 1536], P('dp'), may hold values from -6 to 6
- segment: int32 [8192], P('dp'), may hold values from -1 to 7, as said below
- norm_gain: float32 [1536], replicated, may hold values from 0.5 to 1.5
- gate_weight: bfloat16 [1536, 3072], P(None, 'tensor'), may hold values from -0.15625 to 0.15625
- value_weight: bfloat16 [1536, 3072], P(None, 'tensor'), may hold values from -0.15625 to 0.15625
- state_weight: bfloat16 [1536, 256], replicated, may hold values from -0.15625 to 0.15625
- step_weight: bfloat16 [1536, 48], P(None, 'tensor'), may hold values from -0.15625 to 0.15625
- value_filter: float32 [4, 3072], P(None, 'tensor'), may hold values from -3 to 3
- value_offset: float32 [3072], P('tensor'), may hold values from -3 to 3
- state_filter: float32 [4, 256], replicated, may hold values from -3 to 3
- state_offset: float32 [256], replicated, may hold values from -3 to 3
- step_offset: float32 [48], P('tensor'), may hold values from -6.9 to -2.3
- decay_log: float32 [48], P('tensor'), may hold values from 0 to 2.77
- skip_gain: float32 [48], P('tensor'), may hold values from 0.5 to 1.5
- inner_gain: float32 [3072], P('tensor'), may hold values from 0.1 to 1.9
- output_weight: bfloat16 [3072, 1536], P('tensor'), may hold values from -0.109375 to 0.109375
- cotangent: bfloat16 [8192, 1536], P('dp'), may hold values from -6 to 6
Outputs:
- mixed: bfloat16 [8192, 1536], P('dp', 'tensor')
- tokens_grad: float32 [8192, 1536], P('dp', 'tensor')
- norm_gain_grad: float32 [1536], replicated
- gate_weight_grad: float32 [1536, 3072], P(None, 'tensor')
- value_weight_grad: float32 [1536, 3072], P(None, 'tensor')
- state_weight_grad: float32 [1536, 256], replicated
- step_weight_grad: float32 [1536, 48], P(None, 'tensor')
- value_filter_grad: float32 [4, 3072], P(None, 'tensor')
- value_offset_grad: float32 [3072], P('tensor')
- state_filter_grad: float32 [4, 256], replicated
- state_offset_grad: float32 [256], replicated
- step_offset_grad: float32 [48], P('tensor')
- decay_log_grad: float32 [48], P('tensor')
- skip_gain_grad: float32 [48], P('tensor')
- inner_gain_grad: float32 [3072], P('tensor')
- output_weight_grad: float32 [3072, 1536], P('tensor')
The draws below stay inside these ranges and needn't reach their ends.
Inputs may be any that keep to these rules, and one draw needn't show every extreme that they name: `segment`: within one device's 1024 slots the live tokens come first and the empty slots (id -1) last; a sequence is a run of equal ids among live tokens, ids counting up from 0 along the slots; each has 128 to 1024 tokens except that a device's last live one may be shorter; some device's first sequence has exactly 1024 tokens; each device holds 512 to 1024 live tokens, some device exactly 1024; some device reaches the largest id.
All inputs are finite; a program needn't handle non-finite values.
Results may differ from the reference program's by a relative error of at most 0.0081.
Values sent between devices are 32-bit elements; how exact they have to be, the bound alone decides.
No kernel may reach another device: no remote copies, remote signals or barrier semaphores. Data moves between devices by JAX's collectives and lax.ppermute only.
A program may use at most 192 MiB of HBM per device.

```python
import jax
import jax.numpy as jnp
from jax import lax

D = 1536
INNER = 3072
HEADS = 48
STATE = 128
CONV = 4
BLOCK = 256
SEQ_MAX = 1024
TOK_DEV = 1024
TOKENS = 8192


def draw_segment(key, part):
    groups = TOKENS // TOK_DEV
    slots = TOK_DEV * 8 // SEQ_MAX + 2
    key_len, key_live = jax.random.split(key)
    lengths = jax.random.randint(key_len, (groups, slots), SEQ_MAX // 8, SEQ_MAX + 1)
    index = jnp.arange(groups, dtype=jnp.int32)[:, None]
    first_group = index == 0
    second_group = index == 1
    lengths = jnp.where(first_group | second_group, SEQ_MAX // 8, lengths)
    lengths = jnp.where(first_group & (jnp.arange(slots, dtype=jnp.int32)[None, :] == 0), SEQ_MAX, lengths)
    ends = jnp.cumsum(lengths, axis=1)
    position = jnp.arange(TOK_DEV, dtype=jnp.int32)
    labels = jnp.sum((ends[:, None, :] <= position[None, :, None]).astype(jnp.int32), axis=2)
    live = jax.random.randint(key_live, (groups, 1), SEQ_MAX // 2, TOK_DEV + 1)
    live = jnp.where(first_group | second_group, TOK_DEV, live)
    labels = jnp.where(position[None, :] < live, labels, -1)
    return labels.reshape(-1).astype(jnp.int32)


def block_levels(rng, dims, pieces, low, largest):
    def one(axis_at, blocks):
        steps = jax.random.uniform(jax.random.fold_in(jax.random.fold_in(rng, 6), axis_at), (blocks,), jnp.float32, low / len(pieces), largest / len(pieces))
        return jnp.repeat(jnp.exp(steps), dims[axis_at] // blocks).reshape((-1,) + (1,) * (len(dims) - axis_at - 1))

    level = one(*pieces[0])
    for cut in pieces[1:]:
        level = level * one(*cut)
    return level


def gaussian(rng, shape, scale, reach, pieces=(), held_as=jnp.bfloat16):
    entries = scale * jax.random.normal(rng, shape, jnp.float32)
    if pieces:
        entries = entries * block_levels(rng, shape, pieces, -0.22, 0.18)
    return jnp.clip(entries, -reach, reach).astype(held_as)


def setup_inputs(seed: int = 0) -> dict:
    keys = jax.random.split(jax.random.key(seed), 18)
    return {
        "tokens": gaussian(keys[0], (TOKENS, D), 1.0, 6.0, ((0, 8),)),
        "segment": draw_segment(jax.random.fold_in(keys[17], 71), 0),
        "norm_gain": jnp.clip(1.0 + 0.1 * jax.random.normal(keys[2], (D,), jnp.float32), 0.5, 1.5),
        "gate_weight": gaussian(keys[3], (D, INNER), D ** -0.5, 0.15625, ((1, 4),)),
        "value_weight": gaussian(keys[4], (D, INNER), D ** -0.5, 0.15625, ((1, 4),)),
        "state_weight": gaussian(keys[5], (D, 2 * STATE), D ** -0.5, 0.15625),
        "step_weight": gaussian(keys[6], (D, HEADS), D ** -0.5, 0.15625, ((1, 4),)),
        "value_filter": gaussian(keys[7], (CONV, INNER), CONV ** -0.5, 3.0, ((1, 4),), jnp.float32),
        "value_offset": gaussian(keys[8], (INNER,), 0.5, 3.0, ((0, 4),), jnp.float32),
        "state_filter": gaussian(keys[9], (CONV, 2 * STATE), CONV ** -0.5, 3.0, (), jnp.float32),
        "state_offset": gaussian(keys[10], (2 * STATE,), 0.5, 3.0, (), jnp.float32),
        "step_offset": jnp.clip(-6.9 + 4.6000001430511475 * jax.random.uniform(keys[11], (HEADS,), jnp.float32) ** block_levels(keys[11], (HEADS,), ((0, 4),), -0.2, 0.2), -6.9, -2.3),
        "decay_log": jnp.clip(2.77 * jax.random.uniform(keys[12], (HEADS,), jnp.float32) ** block_levels(keys[12], (HEADS,), ((0, 4),), -0.2, 0.2), 0.0, 2.77),
        "skip_gain": jnp.clip(0.5 + 1.0 * jax.random.uniform(keys[13], (HEADS,), jnp.float32) ** block_levels(keys[13], (HEADS,), ((0, 4),), -0.2, 0.2), 0.5, 1.5),
        "inner_gain": jnp.clip(1.0 + 0.18 * jax.random.normal(keys[14], (INNER,), jnp.float32), 0.1, 1.9),
        "output_weight": gaussian(keys[15], (INNER, D), INNER ** -0.5, 0.109375, ((0, 4),)),
        "cotangent": gaussian(keys[16], (TOKENS, D), 1.0, 6.0, ((0, 8),)),
    }


EPS = 1e-05
HIGH = lax.Precision.HIGHEST

@jax.custom_vjp
def low(v):
    return lax.optimization_barrier(v.astype(jnp.bfloat16)).astype(jnp.float32)

@jax.custom_vjp
def low_back(v):
    return v

def low_keep(v):
    return (low(v), None)

def low_pass(kept, grad):
    return (grad,)

def back_keep(v):
    return (v, None)

def back_low(kept, grad):
    return (low(grad),)
low.defvjp(low_keep, low_pass)
low_back.defvjp(back_keep, back_low)

def product(a, b):
    return jnp.dot(a, b, precision=HIGH, preferred_element_type=jnp.float32)

def causal_filter(signal, segment, weights, offset):
    total = offset[None, :] + weights[0][None, :] * signal
    for back in range(1, CONV):
        moved = jnp.pad(signal, ((back, 0), (0, 0)))[:-back]
        earlier = jnp.pad(segment, (back, 0), constant_values=-2)[:-back]
        keep = (earlier == segment).astype(signal.dtype)
        total = total + weights[back][None, :] * moved * keep[:, None]
    return jax.nn.silu(total)

def mixer(values, enter_map, leave_map, steps, rates, skip_gain, segment):
    length, channels = values.shape
    heads = steps.shape[1]
    width = channels // heads
    blocks = length // BLOCK
    lower = jnp.arange(BLOCK)[:, None] >= jnp.arange(BLOCK)[None, :]
    items = (values.reshape(blocks, BLOCK, heads, width), enter_map.reshape(blocks, BLOCK, -1), leave_map.reshape(blocks, BLOCK, -1), steps.reshape(blocks, BLOCK, heads), rates.reshape(blocks, BLOCK, heads), segment.reshape(blocks, BLOCK))

    def advance(carry, item):
        state, previous = carry
        block_x, block_b, block_c, block_step, block_rate, block_seg = item
        total = jnp.cumsum(block_rate, axis=0)
        across = total.T
        same = ((block_seg[:, None] == block_seg[None, :]) & lower)[None]
        spread = across[:, :, None] - across[:, None, :]
        decay = jnp.where(same, jnp.exp(jnp.where(same, spread, 0.0)), 0.0)
        scores = jnp.dot(block_c, block_b.T, precision=HIGH)
        weights = decay * scores[None] * block_step.T[:, None, :]
        inside = jnp.einsum('hts,shp->thp', weights, block_x, precision=HIGH)
        enter = jnp.exp(total) * (block_seg == previous).astype(values.dtype)[:, None]
        carried = jnp.einsum('tn,hpn->thp', block_c, state, precision=HIGH) * enter[:, :, None]
        last = block_seg[-1]
        tail = jnp.exp(total[-1][None, :] - total) * (block_seg == last).astype(values.dtype)[:, None] * block_step
        keep = jnp.exp(total[-1]) * (last == previous).astype(values.dtype)
        state = state * keep[:, None, None] + jnp.einsum('sh,shp,sn->hpn', tail, block_x, block_b, precision=HIGH)
        return ((state, last), (inside + carried).reshape(BLOCK, channels))
    start = (jnp.zeros((heads, width, enter_map.shape[1]), values.dtype), jnp.array(-3, jnp.int32))
    unused, outputs = lax.scan(jax.checkpoint(advance), start, items)
    return outputs.reshape(length, channels) + values * jnp.repeat(skip_gain, width)[None, :]

def layer(tokens, segment, norm_gain, gate_weight, value_weight, state_weight, step_weight, value_filter, value_offset, state_filter, state_offset, step_offset, decay_log, skip_gain, inner_gain, output_weight):
    scale = lax.rsqrt(lax.optimization_barrier(jnp.mean(tokens * tokens, axis=1, keepdims=True)) + EPS)
    normed = low(tokens * scale * norm_gain[None, :])
    gate = low_back(product(normed, gate_weight))
    values = low_back(product(normed, value_weight))
    states = product(normed, state_weight)
    steps_raw = low_back(product(normed, step_weight))
    mixed_values = causal_filter(values, segment, value_filter, value_offset)
    mixed_states = causal_filter(states, segment, state_filter, state_offset)
    steps = jax.nn.softplus(steps_raw + step_offset[None, :])
    rates = steps * (-jnp.exp(decay_log))[None, :]
    half_state = state_weight.shape[1] // 2
    scanned = mixer(mixed_values, mixed_states[:, :half_state], mixed_states[:, half_state:], steps, rates, skip_gain, segment)
    gated = scanned * jax.nn.silu(gate)
    inner_scale = lax.rsqrt(lax.optimization_barrier(jnp.mean(gated * gated, axis=1, keepdims=True)) + EPS)
    branch = low(gated * inner_scale * inner_gain[None, :])
    live = (segment >= 0).astype(tokens.dtype)
    return tokens + live[:, None] * product(branch, output_weight)

def reference(tokens, segment, norm_gain, gate_weight, value_weight, state_weight, step_weight, value_filter, value_offset, state_filter, state_offset, step_offset, decay_log, skip_gain, inner_gain, output_weight, cotangent):
    floats = tuple((p.astype(jnp.float32) for p in (norm_gain, gate_weight, value_weight, state_weight, step_weight, value_filter, value_offset, state_filter, state_offset, step_offset, decay_log, skip_gain, inner_gain, output_weight)))
    groups = tokens.shape[0] // TOK_DEV
    width = tokens.shape[1]

    def whole(wide, *weights):

        def single(item):
            return layer(item[0], item[1], *weights)
        results = lax.map(jax.checkpoint(single), (wide.reshape(groups, TOK_DEV, width), segment.reshape(groups, TOK_DEV)))
        return results.reshape(groups * TOK_DEV, width)
    result, pullback = jax.vjp(whole, tokens.astype(jnp.float32), *floats)
    grads = pullback(cotangent.astype(jnp.float32))
    return (result.astype(jnp.bfloat16), grads[0], grads[1], grads[2], grads[3], grads[4], grads[5], grads[6], grads[7], grads[8], grads[9], grads[10], grads[11], grads[12], grads[13], grads[14])
```

```python
import jax
import jax.numpy as jnp
from jax import lax
from jax.experimental import pallas as pl
from jax.experimental.pallas import tpu as pltpu
from jax.sharding import PartitionSpec as P

CONV = 4
CHUNK = 128
EPS = 1e-05
HIGH = lax.Precision.HIGHEST
F32 = jnp.float32
BF16 = jnp.bfloat16
FAR = -1e30


def nn(a, b, precision=None):
    return lax.dot_general(
        a, b, (((1,), (0,)), ((), ())), precision=precision, preferred_element_type=F32
    )


def nt(a, b, precision=None):
    return lax.dot_general(
        a, b, (((1,), (1,)), ((), ())), precision=precision, preferred_element_type=F32
    )


def tn(a, b, precision=None):
    return lax.dot_general(
        a, b, (((0,), (0,)), ((), ())), precision=precision, preferred_element_type=F32
    )


def halves(a):
    upper = a.astype(BF16)
    return upper, (a - upper.astype(F32)).astype(BF16)


def sigmoid(v):
    return 0.5 * jnp.tanh(0.5 * v) + 0.5


def softplus(v):
    return jnp.maximum(v, 0.0) + jnp.log1p(jnp.exp(-jnp.abs(v)))


def head_map(heads, channels):
    width = channels // heads
    owner = lax.broadcasted_iota(jnp.int32, (heads, channels), 1) // width
    mine = lax.broadcasted_iota(jnp.int32, (heads, channels), 0)
    return (owner == mine).astype(BF16)


def spread(columns, head_of):
    upper, lower = halves(columns)
    both = jnp.concatenate([upper.astype(F32), lower.astype(F32)], axis=1).astype(BF16)
    return nn(both, jnp.concatenate([head_of, head_of], axis=0))


def gather(wide, head_of):
    upper, lower = halves(wide)
    return nt(upper, head_of) + nt(lower, head_of)


def convolve(ext, signal, before, aux, weights, offset):
    rows = signal.shape[0]
    ext[0:8, :] = before
    ext[8 : 8 + rows, :] = signal
    total = offset + weights[0:1, :] * signal
    for back in range(1, CONV):
        moved = ext[8 - back : 8 - back + rows, :]
        total = total + weights[back : back + 1, :] * (moved * aux[:, back - 1 : back])
    return total


def unfilter(ext, later, sums, grad, signal, aux, weights):
    rows = signal.shape[0]
    ext[0:rows, :] = grad
    ext[rows : rows + 8, :] = later[...]
    later[...] = grad[0:8, :]
    total = weights[0:1, :] * grad
    sums[0:1, :] += jnp.sum(grad * signal, axis=0, keepdims=True)
    for back in range(1, CONV):
        ahead = ext[back : back + rows, :] * aux[:, 2 + back : 3 + back]
        total = total + weights[back : back + 1, :] * ahead
        sums[back : back + 1, :] += jnp.sum(ahead * signal, axis=0, keepdims=True)
    sums[4:5, :] += jnp.sum(grad, axis=0, keepdims=True)
    return total


def triangle(rows):
    down = lax.broadcasted_iota(jnp.int32, (rows, rows), 0)
    along = lax.broadcasted_iota(jnp.int32, (rows, rows), 1)
    return down >= along


def decays(raw, offset, decay, tri):
    moved = raw + offset
    steps = softplus(moved)
    rates = steps * (-jnp.exp(decay))
    total = nn(tri, rates, HIGH)
    total_rows = lax.dot_general(
        rates, tri, (((0,), (1,)), ((), ())), precision=HIGH, preferred_element_type=F32
    )
    return moved, steps, rates, total, total_rows


def forward_kernel(
    ends,
    aux_ref,
    seg_ref,
    u_ref,
    s_ref,
    raw_ref,
    gate_ref,
    bg_ref,
    vf_ref,
    vo_ref,
    sf_ref,
    so_ref,
    off_ref,
    dec_ref,
    skip_ref,
    ig_ref,
    y_ref,
    sum_ref,
    kept_ref,
    uext,
    sext,
    uold,
    sold,
    state,
):
    i = pl.program_id(0)
    rows, channels = u_ref.shape
    heads = raw_ref.shape[1]
    half = s_ref.shape[1] // 2

    @pl.when(i == 0)
    def _():
        uold[...] = jnp.zeros_like(uold)
        sold[...] = jnp.zeros_like(sold)
        state[...] = jnp.zeros_like(state)

    aux = aux_ref[...]
    head_of = head_map(heads, channels)
    u = u_ref[...]
    s = s_ref[...]
    v = convolve(uext, u, uold[...], aux, vf_ref[...], vo_ref[...])
    ms = convolve(sext, s, sold[...], aux, sf_ref[...], so_ref[...])
    uold[...] = u[rows - 8 :, :]
    sold[...] = s[rows - 8 :, :]
    x = v * sigmoid(v)
    ms = ms * sigmoid(ms)
    into = ms[:, :half].astype(BF16)
    out_of = ms[:, half:].astype(BF16)
    lower = triangle(rows)
    tri = lower.astype(F32)
    moved, steps, rates, total, total_rows = decays(raw_ref[...], off_ref[...], dec_ref[...], tri)
    seg_col = aux[:, 6:7]
    seg_row = seg_ref[pl.ds(i, 1), :]
    previous = ends[i]
    last = ends[i + 1]
    far = jnp.where((seg_col == seg_row) & lower, 0.0, FAR)
    scores = nt(out_of, into)
    final = total[rows - 1 :, :]
    enter = jnp.exp(total) * (seg_col == previous).astype(F32)
    tail = jnp.exp(final - total) * (seg_col == last).astype(F32) * steps
    keep = jnp.exp(final) * jnp.where(last == previous, 1.0, 0.0)
    wide = spread(jnp.concatenate([steps, enter, tail, jnp.broadcast_to(keep, (8, heads)),
                                   jnp.broadcast_to(skip_ref[...], (8, heads))], axis=0), head_of)
    step_w = wide[:rows]
    enter_w = wide[rows : 2 * rows]
    tail_w = wide[2 * rows : 3 * rows]
    keep_w = wide[3 * rows : 3 * rows + 1]
    skip_w = wide[3 * rows + 8 : 3 * rows + 9]
    xs = x * step_w
    old = state[...]
    old_low = old.astype(BF16)
    kept_ref[0] = old_low
    carried = nn(out_of, old_low) * enter_w
    state[...] = old * keep_w + tn(into, (x * tail_w).astype(BF16))
    left = lax.broadcasted_iota(jnp.int32, (rows, 128), 1) < 64
    base = carried + skip_w * x
    silu_gate = gate_ref[...]
    silu_gate = silu_gate * sigmoid(silu_gate)
    square = jnp.zeros((rows, 128), F32)
    along = jnp.zeros((rows, 128), F32)
    for pair in range(heads // 2):
        lanes = slice(128 * pair, 128 * pair + 128)
        parts = []
        for h in (2 * pair, 2 * pair + 1):
            gap = (total[:, h : h + 1] - total_rows[h : h + 1, :]) + far
            parts.append((jnp.exp(gap) * scores).astype(BF16))
        xp = xs[:, lanes]
        stacked = jnp.concatenate([jnp.where(left, xp, 0.0), jnp.where(left, 0.0, xp)], axis=0)
        inside = nn(jnp.concatenate(parts, axis=1), stacked.astype(BF16))
        y = inside + base[:, lanes]
        y_ref[:, lanes] = y
        gated = y * silu_gate[:, lanes]
        square = square + gated * gated
        along = along + bg_ref[:, lanes] * ig_ref[:, lanes] * gated
    ones = jnp.ones((8, 128), BF16)
    for index, part in enumerate((square, along)):
        upper, low_part = halves(part)
        sum_ref[index : index + 1, :] = (nt(ones, upper) + nt(ones, low_part))[0:1, :]


def backward_kernel(
    ends,
    aux_ref,
    seg_ref,
    u_ref,
    s_ref,
    raw_ref,
    dy_ref,
    kept_ref,
    vf_ref,
    vo_ref,
    sf_ref,
    so_ref,
    off_ref,
    dec_ref,
    skip_ref,
    ubef_ref,
    sbef_ref,
    du_ref,
    ds_ref,
    draw_ref,
    chan_ref,
    maps_ref,
    head_ref,
    uext,
    sext,
    gext,
    hext,
    glater,
    hlater,
    dstate,
):
    j = pl.program_id(0)
    i = pl.num_programs(0) - 1 - j
    rows, channels = u_ref.shape
    heads = raw_ref.shape[1]
    half = s_ref.shape[1] // 2

    @pl.when(j == 0)
    def _():
        glater[...] = jnp.zeros_like(glater)
        hlater[...] = jnp.zeros_like(hlater)
        maps_ref[...] = jnp.zeros_like(maps_ref)
        dstate[...] = jnp.zeros_like(dstate)
        chan_ref[...] = jnp.zeros_like(chan_ref)
        head_ref[...] = jnp.zeros_like(head_ref)

    aux = aux_ref[...]
    head_of = head_map(heads, channels)
    u = u_ref[...]
    s = s_ref[...]
    first = jnp.where(i == 0, 0.0, 1.0)
    v = convolve(uext, u, ubef_ref[...] * first, aux, vf_ref[...], vo_ref[...])
    ms = convolve(sext, s, sbef_ref[...] * first, aux, sf_ref[...], so_ref[...])
    sig = sigmoid(v)
    x = v * sig
    state_sig = sigmoid(ms)
    ms = ms * state_sig
    into = ms[:, :half].astype(BF16)
    out_of = ms[:, half:].astype(BF16)
    lower = triangle(rows)
    tri = lower.astype(F32)
    moved, steps, rates, total, total_rows = decays(raw_ref[...], off_ref[...], dec_ref[...], tri)
    seg_col = aux[:, 6:7]
    seg_row = seg_ref[pl.ds(i, 1), :]
    previous = ends[i]
    last = ends[i + 1]
    far = jnp.where((seg_col == seg_row) & lower, 0.0, FAR)
    scores = nt(out_of, into)
    final = total[rows - 1 :, :]
    enter = jnp.exp(total) * (seg_col == previous).astype(F32)
    fade = jnp.exp(final - total) * (seg_col == last).astype(F32)
    keep = jnp.exp(final) * jnp.where(last == previous, 1.0, 0.0)
    wide = spread(jnp.concatenate([steps, enter, fade * steps, jnp.broadcast_to(keep, (8, heads)),
                                   jnp.broadcast_to(skip_ref[...], (8, heads))], axis=0), head_of)
    step_w = wide[:rows]
    enter_w = wide[rows : 2 * rows]
    tail_w = wide[2 * rows : 3 * rows]
    keep_w = wide[3 * rows : 3 * rows + 1]
    skip_w = wide[3 * rows + 8 : 3 * rows + 9]
    xs = x * step_w
    dy = dy_ref[...]
    old_low = kept_ref[0]
    after = dstate[...]
    after_low = after.astype(BF16)
    entered = (dy * enter_w).astype(BF16)
    carried = nn(out_of, old_low) * enter_w
    pushed = nn(into, after_low)
    tailed = (x * tail_w).astype(BF16)
    d_out = nt(entered, old_low)
    d_in = nt(tailed, after_low)
    kept_sum = jnp.sum(after * old_low.astype(F32), axis=0, keepdims=True) * keep_w
    dstate[...] = after * keep_w + tn(out_of, entered)
    left = lax.broadcasted_iota(jnp.int32, (rows, 128), 1) < 64
    d_scores = jnp.zeros((rows, rows), F32)
    row_sums = []
    col_sums = []
    pieces = []
    for pair in range(heads // 2):
        lanes = slice(128 * pair, 128 * pair + 128)
        xp = xs[:, lanes].astype(BF16)
        dp = dy[:, lanes]
        d_parts = [jnp.where(left, dp, 0.0).astype(BF16), jnp.where(left, 0.0, dp).astype(BF16)]
        parts = []
        for side in range(2):
            h = 2 * pair + side
            decay = jnp.exp((total[:, h : h + 1] - total_rows[h : h + 1, :]) + far)
            weight = decay * scores
            d_weight = nt(d_parts[side], xp)
            d_scores = d_scores + d_weight * decay
            grown = d_weight * weight
            row_sums.append(jnp.sum(grown, axis=1, keepdims=True))
            col_sums.append(jnp.sum(grown, axis=0, keepdims=True))
            parts.append(weight.astype(BF16))
        pieces.append(tn(jnp.concatenate(parts, axis=0), jnp.concatenate(d_parts, axis=0)))
    dxs = jnp.concatenate(pieces, axis=1)
    d_scores = d_scores.astype(BF16)
    d_maps = jnp.concatenate([d_in + tn(d_scores, out_of), d_out + nn(d_scores, into)], axis=1)
    d_maps = d_maps * (state_sig + ms * (1.0 - state_sig))
    ds_ref[...] = unfilter(hext, hlater, maps_ref, d_maps, s, aux, sf_ref[...])
    dx = dxs * step_w + pushed * tail_w + dy * skip_w
    by_step = gather(dxs * x, head_of)
    by_tail = gather(pushed * x, head_of)
    by_enter = gather(dy * carried, head_of)
    kept_head = gather(jnp.broadcast_to(kept_sum, (8, channels)), head_of)[0:1, :]
    tail_term = by_tail * fade * steps
    d_rows = jnp.concatenate(row_sums, axis=1) + by_enter - tail_term
    d_cols = jnp.concatenate(col_sums, axis=0)
    whole = jnp.sum(tail_term, axis=0, keepdims=True) + kept_head
    d_rates = tn(tri, d_rows, HIGH) - lax.dot_general(
        tri, d_cols, (((0,), (1,)), ((), ())), precision=HIGH, preferred_element_type=F32
    ) + whole
    rate_scale = -jnp.exp(dec_ref[...])
    d_steps = by_step + by_tail * fade + d_rates * rate_scale
    d_raw = d_steps * sigmoid(moved)
    draw_ref[...] = d_raw
    head_ref[0:1, :] += jnp.sum(d_raw, axis=0, keepdims=True)
    head_ref[1:2, :] += jnp.sum(d_rates * rates, axis=0, keepdims=True)
    dv = dx * (sig + x * (1.0 - sig))
    du = unfilter(gext, glater, chan_ref, dv, u, aux, vf_ref[...])
    chan_ref[5:6, :] += jnp.sum(dy * x, axis=0, keepdims=True)
    du_ref[...] = du.astype(BF16)


def side_columns(segment):
    cols = []
    for back in range(1, CONV):
        earlier = jnp.pad(segment, (back, 0), constant_values=-2)[:-back]
        cols.append((earlier == segment).astype(F32))
    for back in range(1, CONV):
        later = jnp.pad(segment, (0, back), constant_values=-2)[back:]
        cols.append((later == segment).astype(F32))
    cols.append(segment.astype(F32))
    cols.append(jnp.zeros_like(cols[0]))
    rows = segment.astype(F32).reshape(-1, CHUNK)
    ends = jnp.concatenate([jnp.full((1,), -3.0, F32), rows[:, -1]])
    return jnp.stack(cols, axis=1), rows, ends


def scan_forward(ends, aux, seg_rows, u, s, raw, gate, bg, vf, vo, sf, so, off, dec, skip, ig):
    length, channels = u.shape
    wide = s.shape[1]
    heads = raw.shape[1]
    half = wide // 2
    blocks = length // CHUNK

    def rowed(n):
        return pl.BlockSpec((CHUNK, n), lambda i: (i, 0))

    def whole(a):
        return pl.BlockSpec(a.shape, lambda i: (0, 0))

    return pl.pallas_call(
        forward_kernel,
        name="scan_forward",
        grid=(blocks,),
        in_specs=[
            pl.BlockSpec(memory_space=pltpu.SMEM),
            rowed(8),
            whole(seg_rows),
            rowed(channels),
            rowed(wide),
            rowed(heads),
            rowed(channels),
            rowed(channels),
            *(whole(a) for a in (vf, vo, sf, so, off, dec, skip, ig)),
        ],
        out_specs=[
            rowed(channels),
            pl.BlockSpec((2, CHUNK), lambda i: (0, i)),
            pl.BlockSpec((1, half, channels), lambda i: (i, 0, 0)),
        ],
        out_shape=[
            jax.ShapeDtypeStruct((length, channels), F32),
            jax.ShapeDtypeStruct((2, length), F32),
            jax.ShapeDtypeStruct((blocks, half, channels), BF16),
        ],
        scratch_shapes=[
            pltpu.VMEM((CHUNK + 8, channels), F32),
            pltpu.VMEM((CHUNK + 8, wide), F32),
            pltpu.VMEM((8, channels), F32),
            pltpu.VMEM((8, wide), F32),
            pltpu.VMEM((half, channels), F32),
        ],
    )(ends, aux, seg_rows, u, s, raw, gate, bg, vf, vo, sf, so, off, dec, skip, ig)


def scan_backward(ends, aux, seg_rows, u, s, raw, dy, kept, vf, vo, sf, so, off, dec, skip):
    length, channels = u.shape
    wide = s.shape[1]
    heads = raw.shape[1]
    half = wide // 2
    blocks = length // CHUNK
    eighths = CHUNK // 8

    def rowed(n):
        return pl.BlockSpec((CHUNK, n), lambda j: (blocks - 1 - j, 0))

    def before(n):
        return pl.BlockSpec((8, n), lambda j: (jnp.maximum((blocks - 1 - j) * eighths - 1, 0), 0))

    def whole(a):
        return pl.BlockSpec(a.shape, lambda j: (0, 0))

    return pl.pallas_call(
        backward_kernel,
        name="scan_backward",
        grid=(blocks,),
        in_specs=[
            pl.BlockSpec(memory_space=pltpu.SMEM),
            rowed(8),
            whole(seg_rows),
            rowed(channels),
            rowed(wide),
            rowed(heads),
            rowed(channels),
            pl.BlockSpec((1, half, channels), lambda j: (blocks - 1 - j, 0, 0)),
            *(whole(a) for a in (vf, vo, sf, so, off, dec, skip)),
            before(channels),
            before(wide),
        ],
        out_specs=[
            rowed(channels),
            rowed(wide),
            rowed(heads),
            pl.BlockSpec((8, channels), lambda j: (0, 0)),
            pl.BlockSpec((8, wide), lambda j: (0, 0)),
            pl.BlockSpec((8, heads), lambda j: (0, 0)),
        ],
        out_shape=[
            jax.ShapeDtypeStruct((length, channels), BF16),
            jax.ShapeDtypeStruct((length, wide), F32),
            jax.ShapeDtypeStruct((length, heads), F32),
            jax.ShapeDtypeStruct((8, channels), F32),
            jax.ShapeDtypeStruct((8, wide), F32),
            jax.ShapeDtypeStruct((8, heads), F32),
        ],
        scratch_shapes=[
            pltpu.VMEM((CHUNK + 8, channels), F32),
            pltpu.VMEM((CHUNK + 8, wide), F32),
            pltpu.VMEM((CHUNK + 8, channels), F32),
            pltpu.VMEM((CHUNK + 8, wide), F32),
            pltpu.VMEM((8, channels), F32),
            pltpu.VMEM((8, wide), F32),
            pltpu.VMEM((half, channels), F32),
        ],
    )(ends, aux, seg_rows, u, s, raw, dy, kept, vf, vo, sf, so, off, dec, skip, u, s)


class Exchange:
    def __init__(self):
        place = lax.axis_index("dp")
        self.side = place & 1
        line = place >> 1
        self.end = (line == 0) | (line == 3)
        self.pair = [(i, i ^ 1) for i in range(8)]
        self.near = [(i, i ^ 2) for i in range(8)]
        self.inward = [(0, 2), (1, 3), (6, 4), (7, 5)]
        self.outward = [(2, 0), (3, 1), (4, 6), (5, 7)]
        self.middle = [(2, 4), (3, 5), (4, 2), (5, 3), (0, 0), (1, 1), (6, 6), (7, 7)]

    def take(self, piece, which):
        rows = piece.shape[0] // 2
        return lax.dynamic_slice_in_dim(piece, which * rows, rows, 0)

    def steps(self, piece):
        half = self.take(piece, self.side) + (yield "pair", self.take(piece, 1 - self.side))
        half = half + (yield "inward", half)
        half = half + (yield "middle", half)
        half = jnp.where(self.end, (yield "outward", half), half)
        other = yield "pair", half
        return jnp.concatenate(
            [jnp.where(self.side == 0, half, other), jnp.where(self.side == 0, other, half)]
        )

    def total(self, pieces):
        live, done, turn = [], [None] * len(pieces), 0
        while turn < len(pieces) or live:
            if turn < len(pieces):
                steps = self.steps(pieces[turn])
                live.append([turn, steps, next(steps)])
            moves = []
            outs = [k for k, item in enumerate(live) if item[2][0] == "outward"]
            for k, item in enumerate(live):
                name, value = item[2]
                if name == "inward":
                    match = [o for o in outs if live[o][2][1].shape == value.shape]
                    if match:
                        outs.remove(match[0])
                        both = jnp.where(self.end, value, live[match[0]][2][1])
                        moves.append(((k, match[0]), both, self.near))
                    else:
                        moves.append(((k,), value, self.inward))
                elif name == "pair":
                    moves.append(((k,), value, self.pair))
                elif name == "middle":
                    moves.append(((k,), value, self.middle))
            moves.extend(((o,), live[o][2][1], self.outward) for o in outs)
            got = lax.optimization_barrier(
                [lax.ppermute(value, "dp", route) for _, value, route in moves]
            )
            result = [None] * len(live)
            for (owners, _, _), value in zip(moves, got):
                for k in owners:
                    result[k] = value
            kept = []
            for item, value in zip(live, result):
                try:
                    item[2] = item[1].send(value)
                    kept.append(item)
                except StopIteration as stop:
                    done[item[0]] = stop.value
            live = kept
            turn += 1
        return done


def total_over_dp(arrays, parts):
    if lax.axis_size("dp") != 8:
        return lax.psum(arrays, "dp")
    pieces = []
    for array, count in zip(arrays, parts):
        rows = array.shape[0] // count
        pieces.extend(array[i * rows : (i + 1) * rows] for i in range(count))
    done = Exchange().total(pieces)
    results = []
    for count in parts:
        results.append(jnp.concatenate(done[:count]) if count > 1 else done[0])
        done = done[count:]
    return results


def on_device(
    tokens,
    segment,
    norm_gain,
    gate_weight,
    value_weight,
    state_weight,
    step_weight,
    value_filter,
    value_offset,
    state_filter,
    state_offset,
    step_offset,
    decay_log,
    skip_gain,
    inner_gain,
    output_weight,
    cotangent,
):
    groups = lax.axis_size("tensor")
    rank = lax.axis_index("tensor")
    channels = inner_gain.shape[0]
    inner_all = channels * groups
    heads = step_offset.shape[0]
    length, width = tokens.shape
    wide_states = state_weight.shape[1]

    wide = tokens.astype(F32)
    scale = lax.rsqrt(jnp.mean(wide * wide, axis=1, keepdims=True) + EPS)
    unit = wide * scale
    normed = (unit * norm_gain[None, :]).astype(BF16)
    live = (segment >= 0).astype(F32)[:, None]
    masked = cotangent * live.astype(BF16)
    gate = nn(normed, gate_weight)
    values = nn(normed, value_weight)
    states = nn(normed, state_weight)
    raw = nn(normed, step_weight)
    branch_grad = nt(masked, output_weight)

    aux, seg_rows, ends = side_columns(segment)
    shared = (
        value_filter,
        value_offset[None, :],
        state_filter,
        state_offset[None, :],
        step_offset[None, :],
        decay_log[None, :],
        skip_gain[None, :],
    )
    scanned, sums, kept = scan_forward(
        ends, aux, seg_rows, values, states, raw, gate, branch_grad, *shared, inner_gain[None, :]
    )
    sums = lax.psum(sums, "tensor") / inner_all
    inner_scale = lax.rsqrt(sums[0] + EPS)
    pull = (inner_scale**3 * sums[1])[:, None]
    inner_scale = inner_scale[:, None]

    gate_sig = jax.nn.sigmoid(gate)
    silu_gate = gate * gate_sig
    gated = scanned * silu_gate
    unit_inner = gated * inner_scale
    branch = (unit_inner * inner_gain[None, :]).astype(BF16)
    gated_grad = inner_scale * (branch_grad * inner_gain[None, :]) - gated * pull
    gate_low = (gated_grad * scanned * (gate_sig + silu_gate * (1.0 - gate_sig))).astype(BF16)
    scanned_grad = gated_grad * silu_gate
    inner_gain_grad = jnp.sum(branch_grad * unit_inner, axis=0)

    output_grad = tn(branch, masked)
    gate_weight_grad = tn(normed, gate_low)
    partial_out = nn(branch, output_weight)
    summed = lax.psum_scatter(partial_out, "tensor", scatter_dimension=1, tiled=True)
    cols = summed.shape[1]
    start = rank * cols
    token_share = lax.dynamic_slice_in_dim(wide, start, cols, 1)
    mixed = (token_share + live * summed).astype(BF16)

    values_low, states_grad, raw_grad, by_channel, by_state, by_head = scan_backward(
        ends, aux, seg_rows, values, states, raw, scanned_grad, kept, *shared
    )
    steps_low = raw_grad.astype(BF16)
    value_weight_grad = tn(normed, values_low)
    states_upper, states_lower = halves(states_grad)
    normed_grad = (
        nt(gate_low, gate_weight)
        + nt(values_low, value_weight)
        + nt(steps_low, step_weight)
        + nt(states_upper, state_weight)
        + nt(states_lower, state_weight)
    )
    state_part = tn(normed, states_upper) + tn(normed, states_lower)
    state_share = lax.psum_scatter(state_part, "tensor", scatter_dimension=0, tiled=True)
    step_weight_grad = tn(steps_low, normed)

    share_grad = lax.psum_scatter(normed_grad, "tensor", scatter_dimension=1, tiled=True)
    along, gain_part, by_state = lax.psum(
        (
            jnp.sum(normed_grad * unit * norm_gain[None, :], axis=1),
            jnp.sum(normed_grad * unit, axis=0),
            by_state,
        ),
        "tensor",
    )
    unit_share = lax.dynamic_slice_in_dim(unit, start, cols, 1)
    gain_share = lax.dynamic_slice_in_dim(norm_gain, start, cols, 0)
    cotangent_share = lax.dynamic_slice_in_dim(cotangent, start, cols, 1).astype(F32)
    tokens_grad = cotangent_share + scale * (
        share_grad * gain_share[None, :] - unit_share * (along / width)[:, None]
    )

    skip_part = jnp.sum(by_channel[5].reshape(heads, -1), axis=1)
    pieces = (
        state_share,
        step_weight_grad,
        gain_part,
        by_channel[:5],
        inner_gain_grad,
        by_state[:5],
        by_head[0],
        by_head[1],
        skip_part,
    )
    sizes = [piece.size for piece in pieces]
    room = -sum(sizes) % (16 * channels)
    extra = jnp.concatenate([piece.reshape(-1) for piece in pieces] + [jnp.zeros((room,), F32)])
    output_grad, gate_weight_grad, value_weight_grad, extra = total_over_dp(
        (output_grad, gate_weight_grad, value_weight_grad, extra.reshape(-1, channels)),
        (3, 3, 3, 1),
    )
    extra = extra.reshape(-1)
    parts = []
    for piece, size in zip(pieces, sizes):
        parts.append(extra[:size].reshape(piece.shape))
        extra = extra[size:]
    state_share, step_grad, gain_grad, chan, inner_grad, state_pair, off, dec, skip = parts
    state_weight_grad = lax.all_gather(state_share, "tensor", axis=0, tiled=True)
    return (
        mixed,
        tokens_grad,
        gain_grad,
        gate_weight_grad,
        value_weight_grad,
        state_weight_grad,
        step_grad.T,
        chan[:4],
        chan[4],
        state_pair[:4],
        state_pair[4],
        off,
        dec,
        skip,
        inner_grad,
        output_grad,
    )


def solution(mesh):
    tokens = P("dp", None)
    columns = P(None, "tensor")
    split = P("tensor")
    return jax.shard_map(
        on_device,
        mesh=mesh,
        in_specs=(
            tokens,
            P("dp"),
            P(),
            columns,
            columns,
            P(),
            columns,
            columns,
            split,
            P(),
            P(),
            split,
            split,
            split,
            split,
            P("tensor", None),
            tokens,
        ),
        out_specs=(
            P("dp", "tensor"),
            P("dp", "tensor"),
            P(),
            columns,
            columns,
            P(),
            columns,
            columns,
            split,
            P(),
            P(),
            split,
            split,
            split,
            split,
            P("tensor", None),
        ),
        check_vma=False,
    )
```

```python
import jax
import jax.numpy as jnp
from jax import lax
from jax.experimental import pallas as pl
from jax.experimental.pallas import tpu as pltpu
from jax.sharding import PartitionSpec as P


CONV = 4
CHUNK = 128
EPS = 1e-05
HIGH = lax.Precision.HIGHEST
F32 = jnp.float32
BF16 = jnp.bfloat16
FAR = -1e30


def nn(a, b, precision=None):
    return lax.dot_general(
        a, b, (((1,), (0,)), ((), ())), precision=precision, preferred_element_type=F32
    )


def nt(a, b, precision=None):
    return lax.dot_general(
        a, b, (((1,), (1,)), ((), ())), precision=precision, preferred_element_type=F32
    )


def tn(a, b, precision=None):
    return lax.dot_general(
        a, b, (((0,), (0,)), ((), ())), precision=precision, preferred_element_type=F32
    )


def halves(a):
    upper = a.astype(BF16)
    return upper, (a - upper.astype(F32)).astype(BF16)


def sigmoid(v):
    return 0.5 * jnp.tanh(0.5 * v) + 0.5


def softplus(v):
    return jnp.maximum(v, 0.0) + jnp.log1p(jnp.exp(-jnp.abs(v)))


def head_map(heads, channels):
    width = channels // heads
    owner = lax.broadcasted_iota(jnp.int32, (heads, channels), 1) // width
    mine = lax.broadcasted_iota(jnp.int32, (heads, channels), 0)
    return (owner == mine).astype(BF16)


def spread(columns, head_of):
    upper, lower = halves(columns)
    both = jnp.concatenate([upper.astype(F32), lower.astype(F32)], axis=1).astype(BF16)
    return nn(both, jnp.concatenate([head_of, head_of], axis=0))


def gather(wide, head_of):
    upper, lower = halves(wide)
    return nt(upper, head_of) + nt(lower, head_of)


def convolve(ext, signal, before, aux, weights, offset):
    rows = signal.shape[0]
    ext[0:8, :] = before
    ext[8 : 8 + rows, :] = signal
    total = offset + weights[0:1, :] * signal
    for back in range(1, CONV):
        moved = ext[8 - back : 8 - back + rows, :]
        total = total + weights[back : back + 1, :] * (moved * aux[:, back - 1 : back])
    return total


def unfilter(ext, later, sums, grad, signal, aux, weights):
    rows = signal.shape[0]
    ext[0:rows, :] = grad
    ext[rows : rows + 8, :] = later[...]
    later[...] = grad[0:8, :]
    total = weights[0:1, :] * grad
    sums[0:1, :] += jnp.sum(grad * signal, axis=0, keepdims=True)
    for back in range(1, CONV):
        ahead = ext[back : back + rows, :] * aux[:, 2 + back : 3 + back]
        total = total + weights[back : back + 1, :] * ahead
        sums[back : back + 1, :] += jnp.sum(ahead * signal, axis=0, keepdims=True)
    sums[4:5, :] += jnp.sum(grad, axis=0, keepdims=True)
    return total


def triangle(rows):
    down = lax.broadcasted_iota(jnp.int32, (rows, rows), 0)
    along = lax.broadcasted_iota(jnp.int32, (rows, rows), 1)
    return down >= along


def decays(raw, offset, decay, tri):
    moved = raw + offset
    steps = softplus(moved)
    rates = steps * (-jnp.exp(decay))
    total = nn(tri, rates, HIGH)
    total_rows = lax.dot_general(
        rates, tri, (((0,), (1,)), ((), ())), precision=HIGH, preferred_element_type=F32
    )
    return moved, steps, rates, total, total_rows


def forward_kernel(
    ends,
    aux_ref,
    seg_ref,
    u_ref,
    s_ref,
    raw_ref,
    gate_ref,
    bg_ref,
    vf_ref,
    vo_ref,
    sf_ref,
    so_ref,
    off_ref,
    dec_ref,
    skip_ref,
    ig_ref,
    y_ref,
    sum_ref,
    kept_ref,
    uext,
    sext,
    uold,
    sold,
    state,
):
    i = pl.program_id(0)
    rows, channels = u_ref.shape
    heads = raw_ref.shape[1]
    half = s_ref.shape[1] // 2

    @pl.when(i == 0)
    def _():
        uold[...] = jnp.zeros_like(uold)
        sold[...] = jnp.zeros_like(sold)
        state[...] = jnp.zeros_like(state)

    aux = aux_ref[...]
    head_of = head_map(heads, channels)
    u = u_ref[...]
    s = s_ref[...]
    v = convolve(uext, u, uold[...], aux, vf_ref[...], vo_ref[...])
    ms = convolve(sext, s, sold[...], aux, sf_ref[...], so_ref[...])
    uold[...] = u[rows - 8 :, :]
    sold[...] = s[rows - 8 :, :]
    x = v * sigmoid(v)
    ms = ms * sigmoid(ms)
    into = ms[:, :half].astype(BF16)
    out_of = ms[:, half:].astype(BF16)
    lower = triangle(rows)
    tri = lower.astype(F32)
    _, steps, _, total, total_rows = decays(raw_ref[...], off_ref[...], dec_ref[...], tri)
    seg_col = aux[:, 6:7]
    seg_row = seg_ref[pl.ds(i, 1), :]
    previous = ends[i]
    last = ends[i + 1]
    far = jnp.where((seg_col == seg_row) & lower, 0.0, FAR)
    scores = nt(out_of, into)
    final = total[rows - 1 :, :]
    enter = jnp.exp(total) * (seg_col == previous).astype(F32)
    tail = jnp.exp(final - total) * (seg_col == last).astype(F32) * steps
    keep = jnp.exp(final) * jnp.where(last == previous, 1.0, 0.0)
    wide = spread(jnp.concatenate([steps, enter, tail, jnp.broadcast_to(keep, (8, heads)),
                                   jnp.broadcast_to(skip_ref[...], (8, heads))], axis=0), head_of)
    step_w = wide[:rows]
    enter_w = wide[rows : 2 * rows]
    tail_w = wide[2 * rows : 3 * rows]
    keep_w = wide[3 * rows : 3 * rows + 1]
    skip_w = wide[3 * rows + 8 : 3 * rows + 9]
    xs = x * step_w
    old = state[...]
    old_low = old.astype(BF16)
    kept_ref[0] = old_low
    carried = nn(out_of, old_low) * enter_w
    state[...] = old * keep_w + tn(into, (x * tail_w).astype(BF16))
    left = lax.broadcasted_iota(jnp.int32, (rows, 128), 1) < 64
    base = carried + skip_w * x
    silu_gate = gate_ref[...]
    silu_gate = silu_gate * sigmoid(silu_gate)
    square = jnp.zeros((rows, 128), F32)
    along = jnp.zeros((rows, 128), F32)
    for pair in range(heads // 2):
        lanes = slice(128 * pair, 128 * pair + 128)
        parts = []
        for h in (2 * pair, 2 * pair + 1):
            gap = (total[:, h : h + 1] - total_rows[h : h + 1, :]) + far
            parts.append((jnp.exp(gap) * scores).astype(BF16))
        xp = xs[:, lanes]
        stacked = jnp.concatenate([jnp.where(left, xp, 0.0), jnp.where(left, 0.0, xp)], axis=0)
        inside = nn(jnp.concatenate(parts, axis=1), stacked.astype(BF16))
        y = inside + base[:, lanes]
        y_ref[:, lanes] = y
        gated = y * silu_gate[:, lanes]
        square = square + gated * gated
        along = along + bg_ref[:, lanes] * ig_ref[:, lanes] * gated
    ones = jnp.ones((8, 128), BF16)
    for index, part in enumerate((square, along)):
        upper, low_part = halves(part)
        sum_ref[index : index + 1, :] = (nt(ones, upper) + nt(ones, low_part))[0:1, :]


def backward_kernel(
    ends,
    aux_ref,
    seg_ref,
    u_ref,
    s_ref,
    raw_ref,
    dy_ref,
    kept_ref,
    vf_ref,
    vo_ref,
    sf_ref,
    so_ref,
    off_ref,
    dec_ref,
    skip_ref,
    ubef_ref,
    sbef_ref,
    du_ref,
    ds_ref,
    dl_ref,
    draw_ref,
    chan_ref,
    maps_ref,
    head_ref,
    uext,
    sext,
    gext,
    hext,
    glater,
    hlater,
    dstate,
):
    j = pl.program_id(0)
    i = pl.num_programs(0) - 1 - j
    rows, channels = u_ref.shape
    heads = raw_ref.shape[1]
    half = s_ref.shape[1] // 2

    @pl.when(j == 0)
    def _():
        glater[...] = jnp.zeros_like(glater)
        hlater[...] = jnp.zeros_like(hlater)
        maps_ref[...] = jnp.zeros_like(maps_ref)
        dstate[...] = jnp.zeros_like(dstate)
        chan_ref[...] = jnp.zeros_like(chan_ref)
        head_ref[...] = jnp.zeros_like(head_ref)

    aux = aux_ref[...]
    head_of = head_map(heads, channels)
    u = u_ref[...]
    s = s_ref[...]
    first = jnp.where(i == 0, 0.0, 1.0)
    v = convolve(uext, u, ubef_ref[...] * first, aux, vf_ref[...], vo_ref[...])
    ms = convolve(sext, s, sbef_ref[...] * first, aux, sf_ref[...], so_ref[...])
    sig = sigmoid(v)
    x = v * sig
    state_sig = sigmoid(ms)
    ms = ms * state_sig
    into = ms[:, :half].astype(BF16)
    out_of = ms[:, half:].astype(BF16)
    lower = triangle(rows)
    tri = lower.astype(F32)
    moved, steps, rates, total, total_rows = decays(raw_ref[...], off_ref[...], dec_ref[...], tri)
    seg_col = aux[:, 6:7]
    seg_row = seg_ref[pl.ds(i, 1), :]
    previous = ends[i]
    last = ends[i + 1]
    far = jnp.where((seg_col == seg_row) & lower, 0.0, FAR)
    scores = nt(out_of, into)
    final = total[rows - 1 :, :]
    enter = jnp.exp(total) * (seg_col == previous).astype(F32)
    fade = jnp.exp(final - total) * (seg_col == last).astype(F32)
    keep = jnp.exp(final) * jnp.where(last == previous, 1.0, 0.0)
    wide = spread(jnp.concatenate([steps, enter, fade * steps, jnp.broadcast_to(keep, (8, heads)),
                                   jnp.broadcast_to(skip_ref[...], (8, heads))], axis=0), head_of)
    step_w = wide[:rows]
    enter_w = wide[rows : 2 * rows]
    tail_w = wide[2 * rows : 3 * rows]
    keep_w = wide[3 * rows : 3 * rows + 1]
    skip_w = wide[3 * rows + 8 : 3 * rows + 9]
    xs = x * step_w
    dy = dy_ref[...]
    old_low = kept_ref[0]
    after = dstate[...]
    after_low = after.astype(BF16)
    entered = (dy * enter_w).astype(BF16)
    carried = nn(out_of, old_low) * enter_w
    pushed = nn(into, after_low)
    tailed = (x * tail_w).astype(BF16)
    d_out = nt(entered, old_low)
    d_in = nt(tailed, after_low)
    kept_sum = jnp.sum(after * old_low.astype(F32), axis=0, keepdims=True) * keep_w
    dstate[...] = after * keep_w + tn(out_of, entered)
    left = lax.broadcasted_iota(jnp.int32, (rows, 128), 1) < 64
    d_scores = jnp.zeros((rows, rows), F32)
    row_sums = []
    col_sums = []
    pieces = []
    for pair in range(heads // 2):
        lanes = slice(128 * pair, 128 * pair + 128)
        xp = xs[:, lanes].astype(BF16)
        dp = dy[:, lanes]
        d_parts = [jnp.where(left, dp, 0.0).astype(BF16), jnp.where(left, 0.0, dp).astype(BF16)]
        parts = []
        for side in range(2):
            h = 2 * pair + side
            decay = jnp.exp((total[:, h : h + 1] - total_rows[h : h + 1, :]) + far)
            weight = decay * scores
            d_weight = nt(d_parts[side], xp)
            d_scores = d_scores + d_weight * decay
            grown = d_weight * weight
            row_sums.append(jnp.sum(grown, axis=1, keepdims=True))
            col_sums.append(jnp.sum(grown, axis=0, keepdims=True))
            parts.append(weight.astype(BF16))
        pieces.append(tn(jnp.concatenate(parts, axis=0), jnp.concatenate(d_parts, axis=0)))
    dxs = jnp.concatenate(pieces, axis=1)
    d_scores = d_scores.astype(BF16)
    d_maps = jnp.concatenate([d_in + tn(d_scores, out_of), d_out + nn(d_scores, into)], axis=1)
    d_maps = d_maps * (state_sig + ms * (1.0 - state_sig))
    ds_ref[...], dl_ref[...] = halves(unfilter(hext, hlater, maps_ref, d_maps, s, aux, sf_ref[...]))
    dx = dxs * step_w + pushed * tail_w + dy * skip_w
    by_step = gather(dxs * x, head_of)
    by_tail = gather(pushed * x, head_of)
    by_enter = gather(dy * carried, head_of)
    kept_head = gather(jnp.broadcast_to(kept_sum, (8, channels)), head_of)[0:1, :]
    tail_term = by_tail * fade * steps
    d_rows = jnp.concatenate(row_sums, axis=1) + by_enter - tail_term
    d_cols = jnp.concatenate(col_sums, axis=0)
    whole = jnp.sum(tail_term, axis=0, keepdims=True) + kept_head
    d_rates = tn(tri, d_rows, HIGH) - lax.dot_general(
        tri, d_cols, (((0,), (1,)), ((), ())), precision=HIGH, preferred_element_type=F32
    ) + whole
    rate_scale = -jnp.exp(dec_ref[...])
    d_steps = by_step + by_tail * fade + d_rates * rate_scale
    d_raw = d_steps * sigmoid(moved)
    draw_ref[...] = d_raw.astype(BF16)
    head_ref[0:1, :] += jnp.sum(d_raw, axis=0, keepdims=True)
    head_ref[1:2, :] += jnp.sum(d_rates * rates, axis=0, keepdims=True)
    dv = dx * (sig + x * (1.0 - sig))
    du = unfilter(gext, glater, chan_ref, dv, u, aux, vf_ref[...])
    chan_ref[5:6, :] += jnp.sum(dy * x, axis=0, keepdims=True)
    du_ref[...] = du.astype(BF16)


def side_columns(segment):
    cols = []
    for back in range(1, CONV):
        earlier = jnp.pad(segment, (back, 0), constant_values=-2)[:-back]
        cols.append((earlier == segment).astype(F32))
    for back in range(1, CONV):
        later = jnp.pad(segment, (0, back), constant_values=-2)[back:]
        cols.append((later == segment).astype(F32))
    cols.append(segment.astype(F32))
    cols.append(jnp.zeros_like(cols[0]))
    rows = segment.astype(F32).reshape(-1, CHUNK)
    ends = jnp.concatenate([jnp.full((1,), -3.0, F32), rows[:, -1]])
    return jnp.stack(cols, axis=1), rows, ends


def scan_forward(ends, aux, seg_rows, u, s, raw, gate, bg, vf, vo, sf, so, off, dec, skip, ig):
    length, channels = u.shape
    wide = s.shape[1]
    heads = raw.shape[1]
    half = wide // 2
    blocks = length // CHUNK

    def rowed(n):
        return pl.BlockSpec((CHUNK, n), lambda i: (i, 0))

    def whole(a):
        return pl.BlockSpec(a.shape, lambda i: (0, 0))

    return pl.pallas_call(
        forward_kernel,
        name="scan_forward",
        cost_estimate=pl.CostEstimate(
            flops=16 * length * channels * (CHUNK + half),
            transcendentals=length * (heads * CHUNK + 3 * channels),
            bytes_accessed=4 * length * (4 * channels + 2 * wide),
        ),
        grid=(blocks,),
        in_specs=[
            pl.BlockSpec(memory_space=pltpu.SMEM),
            rowed(8),
            whole(seg_rows),
            rowed(channels),
            rowed(wide),
            rowed(heads),
            rowed(channels),
            rowed(channels),
            *(whole(a) for a in (vf, vo, sf, so, off, dec, skip, ig)),
        ],
        out_specs=[
            rowed(channels),
            pl.BlockSpec((2, CHUNK), lambda i: (0, i)),
            pl.BlockSpec((1, half, channels), lambda i: (i, 0, 0)),
        ],
        out_shape=[
            jax.ShapeDtypeStruct((length, channels), F32),
            jax.ShapeDtypeStruct((2, length), F32),
            jax.ShapeDtypeStruct((blocks, half, channels), BF16),
        ],
        scratch_shapes=[
            pltpu.VMEM((CHUNK + 8, channels), F32),
            pltpu.VMEM((CHUNK + 8, wide), F32),
            pltpu.VMEM((8, channels), F32),
            pltpu.VMEM((8, wide), F32),
            pltpu.VMEM((half, channels), F32),
        ],
    )(ends, aux, seg_rows, u, s, raw, gate, bg, vf, vo, sf, so, off, dec, skip, ig)


def scan_backward(ends, aux, seg_rows, u, s, raw, dy, kept, vf, vo, sf, so, off, dec, skip):
    length, channels = u.shape
    wide = s.shape[1]
    heads = raw.shape[1]
    half = wide // 2
    blocks = length // CHUNK
    eighths = CHUNK // 8

    def rowed(n):
        return pl.BlockSpec((CHUNK, n), lambda j: (blocks - 1 - j, 0))

    def before(n):
        return pl.BlockSpec((8, n), lambda j: (jnp.maximum((blocks - 1 - j) * eighths - 1, 0), 0))

    def whole(a):
        return pl.BlockSpec(a.shape, lambda j: (0, 0))

    return pl.pallas_call(
        backward_kernel,
        name="scan_backward",
        cost_estimate=pl.CostEstimate(
            flops=40 * length * channels * (CHUNK + half),
            transcendentals=length * (heads * CHUNK + 3 * channels),
            bytes_accessed=4 * length * (4 * channels + 4 * wide),
        ),
        grid=(blocks,),
        in_specs=[
            pl.BlockSpec(memory_space=pltpu.SMEM),
            rowed(8),
            whole(seg_rows),
            rowed(channels),
            rowed(wide),
            rowed(heads),
            rowed(channels),
            pl.BlockSpec((1, half, channels), lambda j: (blocks - 1 - j, 0, 0)),
            *(whole(a) for a in (vf, vo, sf, so, off, dec, skip)),
            before(channels),
            before(wide),
        ],
        out_specs=[
            rowed(channels),
            rowed(wide),
            rowed(wide),
            rowed(heads),
            pl.BlockSpec((8, channels), lambda j: (0, 0)),
            pl.BlockSpec((8, wide), lambda j: (0, 0)),
            pl.BlockSpec((8, heads), lambda j: (0, 0)),
        ],
        out_shape=[
            jax.ShapeDtypeStruct((length, channels), BF16),
            jax.ShapeDtypeStruct((length, wide), BF16),
            jax.ShapeDtypeStruct((length, wide), BF16),
            jax.ShapeDtypeStruct((length, heads), BF16),
            jax.ShapeDtypeStruct((8, channels), F32),
            jax.ShapeDtypeStruct((8, wide), F32),
            jax.ShapeDtypeStruct((8, heads), F32),
        ],
        scratch_shapes=[
            pltpu.VMEM((CHUNK + 8, channels), F32),
            pltpu.VMEM((CHUNK + 8, wide), F32),
            pltpu.VMEM((CHUNK + 8, channels), F32),
            pltpu.VMEM((CHUNK + 8, wide), F32),
            pltpu.VMEM((8, channels), F32),
            pltpu.VMEM((8, wide), F32),
            pltpu.VMEM((half, channels), F32),
        ],
    )(ends, aux, seg_rows, u, s, raw, dy, kept, vf, vo, sf, so, off, dec, skip, u, s)


KINDS = {"O": "AAA", "G": "AAA", "X": "AAA"}
ORDER = (
    "*mo", "*mg", "G1", "O1", "O2", "G0", "O0", "G2", "G1", "*bwd", "*mx", "G1", "O2", "X2",
    "*grad", "O2", "*out", "G0+G1", "*state", "*tot", "X2", "X0", "G0", "O0+O2", "*pack", "X2",
    "X1", "X0+G0", "U", "R", "O2", "U", "O0", "U", "G2+X2", "E", "G1", "U", "F", "O1+O0", "E",
    "G2", "X2", "P", "G0", "F", "O1", "E", "X1+G2", "P", "F", "O0", "R", "P", "E", "O1", "X1",
    "E", "G2", "R", "F", "X0", "O1", "X1", "F", "O0", "O2", "G0", "G1", "G2", "X2", "X0", "X1",
    "P", "E", "O1", "F", "K", "X0", "R", "X1", "K", "K", "X0",
)


class Schedule:
    def __init__(self):
        self.groups = lax.axis_size("tensor")
        place = lax.axis_index("dp")
        self.rank = lax.axis_index("tensor")
        self.side = place & 1
        line = place >> 1
        self.end = (line == 0) | (line == 3)
        self.fold = ((place >> 1) ^ (place >> 2)) & 1
        self.route = {
            "pair": self.routes(lambda i: i ^ 1),
            "near": self.routes(lambda i: i ^ 2),
            "cross": self.routes(lambda i: i ^ 6),
            "middle": self.routes(lambda i: i ^ 6 if 2 <= i < 6 else None),
            "flip": self.routes(lambda i: None),
            "over": [
                (i * self.groups + j, i * self.groups + (j ^ 2))
                for i in range(8)
                for j in range(self.groups)
            ],
        }
        self.last = ()
        self.flows = {}
        self.done = {}

    def routes(self, target):
        pairs = []
        for i in range(8):
            to = target(i)
            for j in range(self.groups):
                there = i * self.groups + (j ^ 1) if to is None else to * self.groups + j
                pairs.append((i * self.groups + j, there))
        return pairs

    def hold(self, values):
        if self.last != ():
            values, self.last = lax.optimization_barrier((values, self.last))
        return values

    def add(self, name, flow):
        self.flows[name] = [flow, None]

    def step(self, names):
        arrived = [self.flows[name][1] for name in names]
        if all(value is not None for value in arrived):
            arrived = self.hold(arrived)
        asked = [self.flows[name][0].send(value) for name, value in zip(names, arrived)]
        if asked[0][0] == "done":
            self.done[names[0]] = asked[0][1]
            return
        route, value = asked[0]
        if len(names) == 2:
            value = jnp.where(self.end, value, asked[1][1])
        got = lax.ppermute(value, ("dp", "tensor"), self.route[route])
        self.last = (value,)
        for name in names:
            self.flows[name][1] = got

    def take(self, piece, which):
        rows = piece.shape[0] // 2
        return lax.dynamic_slice_in_dim(piece, which * rows, rows, 0)

    def join(self, half, other, which):
        return jnp.concatenate(
            [jnp.where(which == 0, half, other), jnp.where(which == 0, other, half)]
        )

    def cut(self, array, first, rows, which):
        return lax.dynamic_slice_in_dim(array, first + which * rows, rows, 0)

    def line_sum(self, array, first, rows):
        array = self.hold(array)
        half = self.cut(array, first, rows // 2, self.side)
        half = half + (yield "pair", self.cut(array, first, rows // 2, 1 - self.side))
        half = half + (yield "near", half)
        half = half + (yield "middle", half)
        half = jnp.where(self.end, (yield "near", half), half)
        yield "done", self.join(half, (yield "pair", half), self.side)

    def fold_sum(self, array, first, rows):
        array = self.hold(array)
        place = lax.axis_index("dp") >> 2
        half = self.cut(array, first, rows // 2, self.fold)
        half = half + (yield "near", self.cut(array, first, rows // 2, 1 - self.fold))
        part = self.take(half, place)
        part = part + (yield "cross", self.take(half, 1 - place))
        part = part + (yield "pair", part)
        half = self.join(part, (yield "cross", part), place)
        yield "done", self.join(half, (yield "near", half), self.fold)

    def scatter(self, array, axis):
        array = self.hold(array)
        size = array.shape[axis] // 4

        def part(which):
            return lax.dynamic_slice_in_dim(array, which * size, size, axis)

        far = yield "flip", part(self.rank ^ 3)
        near = yield "flip", part(self.rank ^ 1)
        over = yield "over", part(self.rank ^ 2) + far
        yield "done", part(self.rank) + near + over

    def gather(self, array):
        array = self.hold(array)
        rows = array.shape[0]
        other = yield "over", array
        pair = jnp.concatenate([array, other])
        crossed = yield "flip", pair
        full = jnp.zeros((4 * rows,) + array.shape[1:], array.dtype)
        for flip, value in zip((0, 2, 1, 3), (array, other, crossed[:rows], crossed[rows:])):
            full = lax.dynamic_update_slice_in_dim(full, value, (self.rank ^ flip) * rows, 0)
        yield "done", full


def on_device(
    tokens,
    segment,
    norm_gain,
    gate_weight,
    value_weight,
    state_weight,
    step_weight,
    value_filter,
    value_offset,
    state_filter,
    state_offset,
    step_offset,
    decay_log,
    skip_gain,
    inner_gain,
    output_weight,
    cotangent,
):
    groups = lax.axis_size("tensor")
    rank = lax.axis_index("tensor")
    channels = inner_gain.shape[0]
    inner_all = channels * groups
    heads = step_offset.shape[0]
    _, width = tokens.shape
    wide_states = state_weight.shape[1]
    cols = width // groups
    start = rank * cols
    cuts = width // channels

    wide = tokens.astype(F32)
    scale = lax.rsqrt(jnp.mean(wide * wide, axis=1, keepdims=True) + EPS)
    normed = (wide * scale * norm_gain[None, :]).astype(BF16)
    live = (segment >= 0).astype(F32)[:, None]
    masked = cotangent * live.astype(BF16)
    gate = nn(normed, gate_weight)
    values = nn(normed, value_weight)
    states = nn(normed, state_weight)
    raw = nn(normed, step_weight)
    branch_grad = nt(masked, output_weight)

    aux, seg_rows, ends = side_columns(segment)
    shared = (
        value_filter,
        value_offset[None, :],
        state_filter,
        state_offset[None, :],
        step_offset[None, :],
        decay_log[None, :],
        skip_gain[None, :],
    )
    scanned, sums, kept = scan_forward(
        ends, aux, seg_rows, values, states, raw, gate, branch_grad, *shared, inner_gain[None, :]
    )
    sums = lax.psum(sums, "tensor") / inner_all
    inner_scale = lax.rsqrt(sums[0] + EPS)
    pull = (inner_scale**3 * sums[1])[:, None]
    inner_scale = inner_scale[:, None]

    gate_sig = jax.nn.sigmoid(gate)
    silu_gate = gate * gate_sig
    gated = scanned * silu_gate
    unit_inner = gated * inner_scale
    branch = (unit_inner * inner_gain[None, :]).astype(BF16)
    gated_grad = inner_scale * (branch_grad * inner_gain[None, :]) - gated * pull
    gate_low = (gated_grad * scanned * (gate_sig + silu_gate * (1.0 - gate_sig))).astype(BF16)
    scanned_grad = gated_grad * silu_gate
    inner_gain_grad = jnp.sum(branch_grad * unit_inner, axis=0)
    env = {}

    def mo(hold):
        env["O"] = tn(branch, masked)
        return env["O"]

    def mg(hold):
        env["G"] = tn(normed, hold(gate_low))
        return env["G"]

    def bwd(hold):
        results = scan_backward(
            ends, aux, seg_rows, values, states, raw, hold(scanned_grad), kept, *shared
        )
        values_low, upper, lower, steps_low, by_channel, by_state, by_head = results
        env["low"] = (values_low, steps_low, upper, lower)
        env["sums"] = (by_channel, by_state, by_head)
        return values_low

    def mx(hold):
        env["X"] = tn(normed, hold(env["low"][0]))
        return env["X"]

    def grad(hold):
        values_low, steps_low, upper, lower = hold(env["low"])
        normed_grad = (
            nt(gate_low, gate_weight)
            + nt(steps_low, step_weight)
            + nt(upper, state_weight)
            + nt(lower, state_weight)
            + nt(values_low, value_weight)
        )
        env["R"] = normed_grad
        unit = hold(tokens).astype(F32) * scale
        env["along"] = jnp.sum(normed_grad * unit * norm_gain[None, :], axis=1)
        env["gain"] = jnp.sum(normed_grad * unit, axis=0)
        return normed_grad, env["along"], env["gain"]

    def state(hold):
        upper, lower = hold(env["low"][2:])
        env["U"] = tn(normed, upper) + tn(normed, lower)
        return env["U"]

    def out(hold):
        env["P"] = nn(hold(branch), output_weight)
        return env["P"]

    def tot(hold):
        env["along"], env["gain"], env["maps"] = lax.psum(
            hold((env["along"], env["gain"], env["sums"][1])), "tensor"
        )
        return env["along"], env["gain"], env["maps"]

    def rows_of(*items):
        laid = []
        for item in items:
            laid.append(jnp.pad(item, ((0, -item.shape[0] % 8), (0, channels - item.shape[1]))))
        return laid

    def pack(hold):
        by_channel, _, by_head = env["sums"]
        skip_part = jnp.sum(by_channel[5].reshape(heads, -1), axis=1)
        small = rows_of(
            by_channel,
            inner_gain_grad[None, :],
            hold(env["maps"]),
            jnp.stack([by_head[0], by_head[1], skip_part]),
        )
        step_grad = tn(env["low"][1], normed)
        for item in (env["gain"][None, :], step_grad):
            small.extend(rows_of(*(item[:, i * channels :][:, :channels] for i in range(cuts))))
        env["heights"] = [item.shape[0] for item in small]
        room = -sum(env["heights"]) % 16
        env["E"] = jnp.concatenate(small + [jnp.zeros((room, channels), F32)])
        return env["E"]

    def mixed_of(summed):
        token_share = lax.dynamic_slice_in_dim(tokens, start, cols, 1).astype(F32)
        return (token_share + live * summed).astype(BF16)

    def tokens_of(share_grad):
        unit_share = lax.dynamic_slice_in_dim(tokens, start, cols, 1).astype(F32) * scale
        gain_share = lax.dynamic_slice_in_dim(norm_gain, start, cols, 0)
        cotangent_share = lax.dynamic_slice_in_dim(cotangent, start, cols, 1).astype(F32)
        return cotangent_share + scale * (
            share_grad * gain_share[None, :] - unit_share * (env["along"] / width)[:, None]
        )

    tasks = dict(mo=mo, mg=mg, bwd=bwd, mx=mx, grad=grad, state=state, out=out, tot=tot, pack=pack)
    if lax.axis_size("dp") != 8 or groups != 4:
        for task in tasks.values():
            task(lambda value: value)
        mixed = mixed_of(lax.psum_scatter(env["P"], "tensor", scatter_dimension=1, tiled=True))
        shared_grad = lax.psum_scatter(env["R"], "tensor", scatter_dimension=1, tiled=True)
        tokens_grad = tokens_of(shared_grad)
        part = lax.psum_scatter(env["U"], "tensor", scatter_dimension=0, tiled=True)
        totals = lax.psum((env["O"], env["G"], env["X"], part, env["E"]), "dp")
        output_grad, gate_weight_grad, value_weight_grad, part, small = totals
        state_weight_grad = lax.all_gather(part, "tensor", axis=0, tiled=True)
    else:
        plan = Schedule()
        for entry in ORDER:
            if entry[0] == "*":
                result = tasks[entry[1:]](plan.hold)
                plan.last = result if isinstance(result, tuple) else (result,)
                continue
            names = entry.split("+")
            for name in names:
                if name in plan.flows:
                    continue
                if name in "PR":
                    flow = plan.scatter(env[name], 1)
                elif name == "U":
                    flow = plan.scatter(env[name], 0)
                elif name == "F":
                    flow = plan.line_sum(plan.done["U"], 0, plan.done["U"].shape[0])
                elif name == "K":
                    flow = plan.gather(plan.done["F"])
                elif name == "E":
                    flow = plan.line_sum(env["E"], 0, env["E"].shape[0])
                else:
                    kinds, array = KINDS[name[0]], env[name[0]]
                    rows, i = array.shape[0] // len(kinds), int(name[1])
                    flow = plan.line_sum if kinds[i] == "A" else plan.fold_sum
                    flow = flow(array, i * rows, rows)
                plan.add(name, flow)
            plan.step(names)
        mixed = mixed_of(plan.done["P"])
        tokens_grad = tokens_of(plan.done["R"])
        state_weight_grad = plan.done["K"]
        output_grad, gate_weight_grad, value_weight_grad = (
            jnp.concatenate([plan.done[f"{key}{i}"] for i in range(len(KINDS[key]))])
            for key in "OGX"
        )
        small = plan.done["E"]
    parts = []
    for height in env["heights"]:
        parts.append(small[:height])
        small = small[height:]
    chan, inner_grad, state_pair, head = parts[:4]
    gain_grad = jnp.concatenate([part[0] for part in parts[4 : 4 + cuts]])
    step_grad = jnp.concatenate([part[:heads] for part in parts[4 + cuts :]], axis=1)
    state_pair = state_pair[:, :wide_states]
    off, dec, skip = (head[i, :heads] for i in range(3))
    return (
        mixed,
        tokens_grad,
        gain_grad,
        gate_weight_grad,
        value_weight_grad,
        state_weight_grad,
        step_grad.T,
        chan[:4],
        chan[4],
        state_pair[:4],
        state_pair[4],
        off,
        dec,
        skip,
        inner_grad[0],
        output_grad,
    )


def solution(mesh):
    tokens = P("dp", None)
    columns = P(None, "tensor")
    split = P("tensor")

    return jax.shard_map(
        on_device,
        mesh=mesh,
        in_specs=(
            tokens,
            P("dp"),
            P(),
            columns,
            columns,
            P(),
            columns,
            columns,
            split,
            P(),
            P(),
            split,
            split,
            split,
            split,
            P("tensor", None),
            tokens,
        ),
        out_specs=(
            P("dp", "tensor"),
            P("dp", "tensor"),
            P(),
            columns,
            columns,
            P(),
            columns,
            columns,
            split,
            P(),
            P(),
            split,
            split,
            split,
            split,
            P("tensor", None),
        ),
        check_vma=False,
    )
```

```python
import jax
import jax.numpy as jnp
from jax import lax
from jax.experimental import pallas as pl
from jax.experimental.pallas import tpu as pltpu
from jax.sharding import PartitionSpec as P


CONV = 4
CHUNK = 128
EPS = 1e-05
HIGH = lax.Precision.HIGHEST
F32 = jnp.float32
BF16 = jnp.bfloat16
FAR = -1e30


def nn(a, b, precision=None):
    return lax.dot_general(
        a, b, (((1,), (0,)), ((), ())), precision=precision, preferred_element_type=F32
    )


def nt(a, b, precision=None):
    return lax.dot_general(
        a, b, (((1,), (1,)), ((), ())), precision=precision, preferred_element_type=F32
    )


def tn(a, b, precision=None):
    return lax.dot_general(
        a, b, (((0,), (0,)), ((), ())), precision=precision, preferred_element_type=F32
    )


def halves(a):
    upper = a.astype(BF16)
    return upper, (a - upper.astype(F32)).astype(BF16)


def sigmoid(v):
    return 0.5 * jnp.tanh(0.5 * v) + 0.5


def softplus(v):
    return jnp.maximum(v, 0.0) + jnp.log1p(jnp.exp(-jnp.abs(v)))


def head_map(heads, channels):
    width = channels // heads
    owner = lax.broadcasted_iota(jnp.int32, (heads, channels), 1) // width
    mine = lax.broadcasted_iota(jnp.int32, (heads, channels), 0)
    return (owner == mine).astype(BF16)


def spread(columns, head_of):
    upper, lower = halves(columns)
    both = jnp.concatenate([upper.astype(F32), lower.astype(F32)], axis=1).astype(BF16)
    return nn(both, jnp.concatenate([head_of, head_of], axis=0))


def gather(wide, head_of):
    upper, lower = halves(wide)
    return nt(upper, head_of) + nt(lower, head_of)


def convolve(ext, signal, before, aux, weights, offset):
    rows = signal.shape[0]
    ext[0:8, :] = before
    ext[8 : 8 + rows, :] = signal
    total = offset + weights[0:1, :] * signal
    for back in range(1, CONV):
        moved = ext[8 - back : 8 - back + rows, :]
        total = total + weights[back : back + 1, :] * (moved * aux[:, back - 1 : back])
    return total


def unfilter(ext, later, sums, grad, signal, aux, weights):
    rows = signal.shape[0]
    ext[0:rows, :] = grad
    ext[rows : rows + 8, :] = later[...]
    later[...] = grad[0:8, :]
    total = weights[0:1, :] * grad
    sums[0:1, :] += jnp.sum(grad * signal, axis=0, keepdims=True)
    for back in range(1, CONV):
        ahead = ext[back : back + rows, :] * aux[:, 2 + back : 3 + back]
        total = total + weights[back : back + 1, :] * ahead
        sums[back : back + 1, :] += jnp.sum(ahead * signal, axis=0, keepdims=True)
    sums[4:5, :] += jnp.sum(grad, axis=0, keepdims=True)
    return total


def triangle(rows):
    down = lax.broadcasted_iota(jnp.int32, (rows, rows), 0)
    along = lax.broadcasted_iota(jnp.int32, (rows, rows), 1)
    return down >= along


def decays(raw, offset, decay, tri):
    moved = raw + offset
    steps = softplus(moved)
    rates = steps * (-jnp.exp(decay))
    total = nn(tri, rates, HIGH)
    total_rows = lax.dot_general(
        rates, tri, (((0,), (1,)), ((), ())), precision=HIGH, preferred_element_type=F32
    )
    return moved, steps, rates, total, total_rows


def front_kernel(
    live_ref,
    tokens_ref,
    cot_ref,
    gain_ref,
    gate_w,
    value_w,
    state_w,
    step_w,
    out_w,
    normed_ref,
    gate_ref,
    value_ref,
    state_ref,
    step_ref,
    masked_ref,
    bg_ref,
):
    wide = tokens_ref[...].astype(F32)
    scale = lax.rsqrt(jnp.mean(wide * wide, axis=1, keepdims=True) + EPS)
    normed = (wide * scale * gain_ref[...][None, :]).astype(BF16)
    normed_ref[...] = normed
    live = (live_ref[:, 6:7] >= 0.0).astype(F32)
    masked = (cot_ref[...].astype(F32) * live).astype(BF16)
    masked_ref[...] = masked
    value_ref[...] = nn(normed, value_w[...])
    state_ref[...] = nn(normed, state_w[...])
    step_ref[...] = nt(normed, step_w[...])
    gate_ref[...] = nn(normed, gate_w[...])
    bg_ref[...] = nt(masked, out_w[...])


def front(aux, tokens, cotangent, gain, gate_w, value_w, state_w, step_w, out_w):
    length, width = tokens.shape
    rows = 256
    channels, wide, heads = gate_w.shape[1], state_w.shape[1], step_w.shape[0]

    def rowed(n):
        return pl.BlockSpec((rows, n), lambda i: (i, 0))

    def whole(a):
        return pl.BlockSpec(a.shape, lambda i: (0,) * a.ndim)

    return pl.pallas_call(
        front_kernel,
        name="front",
        grid=(length // rows,),
        in_specs=[
            rowed(8),
            rowed(width),
            rowed(width),
            *(whole(a) for a in (gain, gate_w, value_w, state_w, step_w, out_w)),
        ],
        out_specs=[
            rowed(width),
            rowed(channels),
            rowed(channels),
            rowed(wide),
            rowed(heads),
            rowed(width),
            rowed(channels),
        ],
        out_shape=[
            jax.ShapeDtypeStruct((length, width), BF16),
            jax.ShapeDtypeStruct((length, channels), F32),
            jax.ShapeDtypeStruct((length, channels), F32),
            jax.ShapeDtypeStruct((length, wide), F32),
            jax.ShapeDtypeStruct((length, heads), F32),
            jax.ShapeDtypeStruct((length, width), BF16),
            jax.ShapeDtypeStruct((length, channels), F32),
        ],
    )(aux, tokens, cotangent, gain, gate_w, value_w, state_w, step_w, out_w)


def forward_kernel(
    ends,
    aux_ref,
    seg_ref,
    u_ref,
    s_ref,
    raw_ref,
    gate_ref,
    bg_ref,
    vf_ref,
    vo_ref,
    sf_ref,
    so_ref,
    off_ref,
    dec_ref,
    skip_ref,
    ig_ref,
    y_ref,
    sum_ref,
    kept_ref,
    uext,
    sext,
    uold,
    sold,
    state,
):
    i = pl.program_id(0)
    rows, channels = u_ref.shape
    heads = raw_ref.shape[1]
    half = s_ref.shape[1] // 2

    @pl.when(i == 0)
    def _():
        uold[...] = jnp.zeros_like(uold)
        sold[...] = jnp.zeros_like(sold)
        state[...] = jnp.zeros_like(state)

    aux = aux_ref[...]
    head_of = head_map(heads, channels)
    u = u_ref[...]
    s = s_ref[...]
    v = convolve(uext, u, uold[...], aux, vf_ref[...], vo_ref[...][None, :])
    ms = convolve(sext, s, sold[...], aux, sf_ref[...], so_ref[...][None, :])
    uold[...] = u[rows - 8 :, :]
    sold[...] = s[rows - 8 :, :]
    x = v * sigmoid(v)
    ms = ms * sigmoid(ms)
    into = ms[:, :half].astype(BF16)
    out_of = ms[:, half:].astype(BF16)
    lower = triangle(rows)
    tri = lower.astype(F32)
    _, steps, _, total, total_rows = decays(raw_ref[...], off_ref[...][None, :], dec_ref[...][None, :], tri)
    seg_col = aux[:, 6:7]
    seg_row = seg_ref[pl.ds(i, 1), :]
    previous = ends[i]
    last = ends[i + 1]
    far = jnp.where((seg_col == seg_row) & lower, 0.0, FAR)
    scores = nt(out_of, into)
    final = total[rows - 1 :, :]
    enter = jnp.exp(total) * (seg_col == previous).astype(F32)
    tail = jnp.exp(final - total) * (seg_col == last).astype(F32) * steps
    keep = jnp.exp(final) * jnp.where(last == previous, 1.0, 0.0)
    wide = spread(jnp.concatenate([steps, enter, tail, jnp.broadcast_to(keep, (8, heads)),
                                   jnp.broadcast_to(skip_ref[...][None, :], (8, heads))], axis=0), head_of)
    step_w = wide[:rows]
    enter_w = wide[rows : 2 * rows]
    tail_w = wide[2 * rows : 3 * rows]
    keep_w = wide[3 * rows : 3 * rows + 1]
    skip_w = wide[3 * rows + 8 : 3 * rows + 9]
    xs = x * step_w
    old = state[...]
    old_low = old.astype(BF16)
    kept_ref[0] = old_low
    carried = nn(out_of, old_low) * enter_w
    state[...] = old * keep_w + tn(into, (x * tail_w).astype(BF16))
    left = lax.broadcasted_iota(jnp.int32, (rows, 128), 1) < 64
    base = carried + skip_w * x
    silu_gate = gate_ref[...]
    silu_gate = silu_gate * sigmoid(silu_gate)
    ig = ig_ref[...][None, :]
    square = jnp.zeros((rows, 128), F32)
    along = jnp.zeros((rows, 128), F32)
    for pair in range(heads // 2):
        lanes = slice(128 * pair, 128 * pair + 128)
        parts = []
        for h in (2 * pair, 2 * pair + 1):
            gap = (total[:, h : h + 1] - total_rows[h : h + 1, :]) + far
            parts.append((jnp.exp(gap) * scores).astype(BF16))
        xp = xs[:, lanes]
        stacked = jnp.concatenate([jnp.where(left, xp, 0.0), jnp.where(left, 0.0, xp)], axis=0)
        inside = nn(jnp.concatenate(parts, axis=1), stacked.astype(BF16))
        y = inside + base[:, lanes]
        y_ref[:, lanes] = y
        gated = y * silu_gate[:, lanes]
        square = square + gated * gated
        along = along + bg_ref[:, lanes] * ig[:, lanes] * gated
    ones = jnp.ones((8, 128), BF16)
    for index, part in enumerate((square, along)):
        upper, low_part = halves(part)
        sum_ref[index : index + 1, :] = (nt(ones, upper) + nt(ones, low_part))[0:1, :]


def backward_kernel(
    ends,
    aux_ref,
    seg_ref,
    u_ref,
    s_ref,
    raw_ref,
    dy_ref,
    kept_ref,
    vf_ref,
    vo_ref,
    sf_ref,
    so_ref,
    off_ref,
    dec_ref,
    skip_ref,
    ubef_ref,
    sbef_ref,
    du_ref,
    ds_ref,
    dl_ref,
    draw_ref,
    chan_ref,
    maps_ref,
    head_ref,
    uext,
    sext,
    gext,
    hext,
    glater,
    hlater,
    dstate,
):
    j = pl.program_id(0)
    i = pl.num_programs(0) - 1 - j
    rows, channels = u_ref.shape
    heads = raw_ref.shape[1]
    half = s_ref.shape[1] // 2

    @pl.when(j == 0)
    def _():
        glater[...] = jnp.zeros_like(glater)
        hlater[...] = jnp.zeros_like(hlater)
        maps_ref[...] = jnp.zeros_like(maps_ref)
        dstate[...] = jnp.zeros_like(dstate)
        chan_ref[...] = jnp.zeros_like(chan_ref)
        head_ref[...] = jnp.zeros_like(head_ref)

    aux = aux_ref[...]
    head_of = head_map(heads, channels)
    u = u_ref[...]
    s = s_ref[...]
    first = jnp.where(i == 0, 0.0, 1.0)
    v = convolve(uext, u, ubef_ref[...] * first, aux, vf_ref[...], vo_ref[...][None, :])
    ms = convolve(sext, s, sbef_ref[...] * first, aux, sf_ref[...], so_ref[...][None, :])
    sig = sigmoid(v)
    x = v * sig
    state_sig = sigmoid(ms)
    ms = ms * state_sig
    into = ms[:, :half].astype(BF16)
    out_of = ms[:, half:].astype(BF16)
    lower = triangle(rows)
    tri = lower.astype(F32)
    moved, steps, rates, total, total_rows = decays(raw_ref[...], off_ref[...][None, :], dec_ref[...][None, :], tri)
    seg_col = aux[:, 6:7]
    seg_row = seg_ref[pl.ds(i, 1), :]
    previous = ends[i]
    last = ends[i + 1]
    far = jnp.where((seg_col == seg_row) & lower, 0.0, FAR)
    scores = nt(out_of, into)
    final = total[rows - 1 :, :]
    enter = jnp.exp(total) * (seg_col == previous).astype(F32)
    fade = jnp.exp(final - total) * (seg_col == last).astype(F32)
    keep = jnp.exp(final) * jnp.where(last == previous, 1.0, 0.0)
    wide = spread(jnp.concatenate([steps, enter, fade * steps, jnp.broadcast_to(keep, (8, heads)),
                                   jnp.broadcast_to(skip_ref[...][None, :], (8, heads))], axis=0), head_of)
    step_w = wide[:rows]
    enter_w = wide[rows : 2 * rows]
    tail_w = wide[2 * rows : 3 * rows]
    keep_w = wide[3 * rows : 3 * rows + 1]
    skip_w = wide[3 * rows + 8 : 3 * rows + 9]
    xs = x * step_w
    dy = dy_ref[...]
    old_low = kept_ref[0]
    after = dstate[...]
    after_low = after.astype(BF16)
    entered = (dy * enter_w).astype(BF16)
    carried = nn(out_of, old_low) * enter_w
    pushed = nn(into, after_low)
    tailed = (x * tail_w).astype(BF16)
    d_out = nt(entered, old_low)
    d_in = nt(tailed, after_low)
    kept_sum = jnp.sum(after * old_low.astype(F32), axis=0, keepdims=True) * keep_w
    dstate[...] = after * keep_w + tn(out_of, entered)
    left = lax.broadcasted_iota(jnp.int32, (rows, 128), 1) < 64
    d_scores = jnp.zeros((rows, rows), F32)
    row_sums = []
    col_sums = []
    pieces = []
    for pair in range(heads // 2):
        lanes = slice(128 * pair, 128 * pair + 128)
        xp = xs[:, lanes].astype(BF16)
        dp = dy[:, lanes]
        d_parts = [jnp.where(left, dp, 0.0).astype(BF16), jnp.where(left, 0.0, dp).astype(BF16)]
        parts = []
        for side in range(2):
            h = 2 * pair + side
            decay = jnp.exp((total[:, h : h + 1] - total_rows[h : h + 1, :]) + far)
            weight = decay * scores
            d_weight = nt(d_parts[side], xp)
            d_scores = d_scores + d_weight * decay
            grown = d_weight * weight
            row_sums.append(jnp.sum(grown, axis=1, keepdims=True))
            col_sums.append(jnp.sum(grown, axis=0, keepdims=True))
            parts.append(weight.astype(BF16))
        pieces.append(tn(jnp.concatenate(parts, axis=0), jnp.concatenate(d_parts, axis=0)))
    dxs = jnp.concatenate(pieces, axis=1)
    d_scores = d_scores.astype(BF16)
    d_maps = jnp.concatenate([d_in + tn(d_scores, out_of), d_out + nn(d_scores, into)], axis=1)
    d_maps = d_maps * (state_sig + ms * (1.0 - state_sig))
    ds_ref[...], dl_ref[...] = halves(unfilter(hext, hlater, maps_ref, d_maps, s, aux, sf_ref[...]))
    dx = dxs * step_w + pushed * tail_w + dy * skip_w
    by_step = gather(dxs * x, head_of)
    by_tail = gather(pushed * x, head_of)
    by_enter = gather(dy * carried, head_of)
    kept_head = gather(jnp.broadcast_to(kept_sum, (8, channels)), head_of)[0:1, :]
    tail_term = by_tail * fade * steps
    d_rows = jnp.concatenate(row_sums, axis=1) + by_enter - tail_term
    d_cols = jnp.concatenate(col_sums, axis=0)
    whole = jnp.sum(tail_term, axis=0, keepdims=True) + kept_head
    d_rates = tn(tri, d_rows, HIGH) - lax.dot_general(
        tri, d_cols, (((0,), (1,)), ((), ())), precision=HIGH, preferred_element_type=F32
    ) + whole
    rate_scale = -jnp.exp(dec_ref[...][None, :])
    d_steps = by_step + by_tail * fade + d_rates * rate_scale
    d_raw = d_steps * sigmoid(moved)
    draw_ref[...] = d_raw.astype(BF16)
    head_ref[0:1, :] += jnp.sum(d_raw, axis=0, keepdims=True)
    head_ref[1:2, :] += jnp.sum(d_rates * rates, axis=0, keepdims=True)
    dv = dx * (sig + x * (1.0 - sig))
    du = unfilter(gext, glater, chan_ref, dv, u, aux, vf_ref[...])
    chan_ref[5:6, :] += jnp.sum(dy * x, axis=0, keepdims=True)
    du_ref[...] = du.astype(BF16)


def side_columns(segment):
    cols = []
    for back in range(1, CONV):
        earlier = jnp.pad(segment, (back, 0), constant_values=-2)[:-back]
        cols.append((earlier == segment).astype(F32))
    for back in range(1, CONV):
        later = jnp.pad(segment, (0, back), constant_values=-2)[back:]
        cols.append((later == segment).astype(F32))
    cols.append(segment.astype(F32))
    cols.append(jnp.zeros_like(cols[0]))
    rows = segment.astype(F32).reshape(-1, CHUNK)
    ends = jnp.concatenate([jnp.full((1,), -3.0, F32), rows[:, -1]])
    return jnp.stack(cols, axis=1), rows, ends


def scan_forward(ends, aux, seg_rows, u, s, raw, gate, bg, vf, vo, sf, so, off, dec, skip, ig):
    length, channels = u.shape
    wide = s.shape[1]
    heads = raw.shape[1]
    half = wide // 2
    blocks = length // CHUNK

    def rowed(n):
        return pl.BlockSpec((CHUNK, n), lambda i: (i, 0))

    def whole(a):
        return pl.BlockSpec(a.shape, lambda i: (0,) * a.ndim)

    return pl.pallas_call(
        forward_kernel,
        name="scan_forward",
        cost_estimate=pl.CostEstimate(
            flops=16 * length * channels * (CHUNK + half),
            transcendentals=length * (heads * CHUNK + 3 * channels),
            bytes_accessed=4 * length * (4 * channels + 2 * wide),
        ),
        grid=(blocks,),
        in_specs=[
            pl.BlockSpec(memory_space=pltpu.SMEM),
            rowed(8),
            whole(seg_rows),
            rowed(channels),
            rowed(wide),
            rowed(heads),
            rowed(channels),
            rowed(channels),
            *(whole(a) for a in (vf, vo, sf, so, off, dec, skip, ig)),
        ],
        out_specs=[
            rowed(channels),
            pl.BlockSpec((2, CHUNK), lambda i: (0, i)),
            pl.BlockSpec((1, half, channels), lambda i: (i, 0, 0)),
        ],
        out_shape=[
            jax.ShapeDtypeStruct((length, channels), F32),
            jax.ShapeDtypeStruct((2, length), F32),
            jax.ShapeDtypeStruct((blocks, half, channels), BF16),
        ],
        scratch_shapes=[
            pltpu.VMEM((CHUNK + 8, channels), F32),
            pltpu.VMEM((CHUNK + 8, wide), F32),
            pltpu.VMEM((8, channels), F32),
            pltpu.VMEM((8, wide), F32),
            pltpu.VMEM((half, channels), F32),
        ],
    )(ends, aux, seg_rows, u, s, raw, gate, bg, vf, vo, sf, so, off, dec, skip, ig)


def scan_backward(ends, aux, seg_rows, u, s, raw, dy, kept, vf, vo, sf, so, off, dec, skip):
    length, channels = u.shape
    wide = s.shape[1]
    heads = raw.shape[1]
    half = wide // 2
    blocks = length // CHUNK
    eighths = CHUNK // 8

    def rowed(n):
        return pl.BlockSpec((CHUNK, n), lambda j: (blocks - 1 - j, 0))

    def before(n):
        return pl.BlockSpec((8, n), lambda j: (jnp.maximum((blocks - 1 - j) * eighths - 1, 0), 0))

    def whole(a):
        return pl.BlockSpec(a.shape, lambda j: (0,) * a.ndim)

    return pl.pallas_call(
        backward_kernel,
        name="scan_backward",
        cost_estimate=pl.CostEstimate(
            flops=40 * length * channels * (CHUNK + half),
            transcendentals=length * (heads * CHUNK + 3 * channels),
            bytes_accessed=4 * length * (4 * channels + 4 * wide),
        ),
        grid=(blocks,),
        in_specs=[
            pl.BlockSpec(memory_space=pltpu.SMEM),
            rowed(8),
            whole(seg_rows),
            rowed(channels),
            rowed(wide),
            rowed(heads),
            rowed(channels),
            pl.BlockSpec((1, half, channels), lambda j: (blocks - 1 - j, 0, 0)),
            *(whole(a) for a in (vf, vo, sf, so, off, dec, skip)),
            before(channels),
            before(wide),
        ],
        out_specs=[
            rowed(channels),
            rowed(wide),
            rowed(wide),
            rowed(heads),
            pl.BlockSpec((8, channels), lambda j: (0, 0)),
            pl.BlockSpec((8, wide), lambda j: (0, 0)),
            pl.BlockSpec((8, heads), lambda j: (0, 0)),
        ],
        out_shape=[
            jax.ShapeDtypeStruct((length, channels), BF16),
            jax.ShapeDtypeStruct((length, wide), BF16),
            jax.ShapeDtypeStruct((length, wide), BF16),
            jax.ShapeDtypeStruct((length, heads), BF16),
            jax.ShapeDtypeStruct((8, channels), F32),
            jax.ShapeDtypeStruct((8, wide), F32),
            jax.ShapeDtypeStruct((8, heads), F32),
        ],
        scratch_shapes=[
            pltpu.VMEM((CHUNK + 8, channels), F32),
            pltpu.VMEM((CHUNK + 8, wide), F32),
            pltpu.VMEM((CHUNK + 8, channels), F32),
            pltpu.VMEM((CHUNK + 8, wide), F32),
            pltpu.VMEM((8, channels), F32),
            pltpu.VMEM((8, wide), F32),
            pltpu.VMEM((half, channels), F32),
        ],
    )(ends, aux, seg_rows, u, s, raw, dy, kept, vf, vo, sf, so, off, dec, skip, u, s)


KINDS = {"O": "A3", "G": "A3", "X": "A3"}
ORDER = (
    "*so", "O", "*ko", "*sg", "*bwd", "*state", "G", "U", "O2", "U", "O1", "U", "*grad", "U",
    "O0", "O2", "*sx", "X", "O1", "*kg", "G2", "*kx", "O0", "G1+O2", "*tot", "G2", "G0+O1",
    "O2", "*pack", "X1+O0", "E", "G0", "O1", "X0+G2", "R", "O0", "G1", "E", "X2+G0", "X1",
    "G2", "R", "*out", "E", "G1", "G0", "P", "R", "X2", "E", "G1", "X1", "X0", "P", "O2", "E",
    "X2", "X1", "E", "K", "P", "X0", "X2", "O0", "O1", "X1", "G2", "G0", "X0", "K", "G1", "X2",
    "R", "K", "P", "X0",
)


class Schedule:
    def __init__(self):
        self.groups = lax.axis_size("tensor")
        place = lax.axis_index("dp")
        self.rank = lax.axis_index("tensor")
        self.side = place & 1
        line = place >> 1
        self.end = (line == 0) | (line == 3)
        self.fold = ((place >> 1) ^ (place >> 2)) & 1
        self.route = {
            "pair": self.routes(lambda i: i ^ 1),
            "near": self.routes(lambda i: i ^ 2),
            "cross": self.routes(lambda i: i ^ 6),
            "middle": self.routes(lambda i: i ^ 6 if 2 <= i < 6 else None),
            "flip": self.routes(lambda i: None),
            "over": [
                (i * self.groups + j, i * self.groups + (j ^ 2))
                for i in range(8)
                for j in range(self.groups)
            ],
        }
        self.last = ()
        self.flows = {}
        self.done = {}

    def routes(self, target):
        pairs = []
        for i in range(8):
            to = target(i)
            for j in range(self.groups):
                there = i * self.groups + (j ^ 1) if to is None else to * self.groups + j
                pairs.append((i * self.groups + j, there))
        return pairs

    def hold(self, values):
        if self.last != ():
            values, self.last = lax.optimization_barrier((values, self.last))
        return values

    def add(self, name, flow):
        self.flows[name] = [flow, None]

    def step(self, names):
        arrived = [self.flows[name][1] for name in names]
        if all(value is not None for value in arrived):
            arrived = self.hold(arrived)
        asked = [self.flows[name][0].send(value) for name, value in zip(names, arrived)]
        if asked[0][0] == "done":
            self.done[names[0]] = asked[0][1]
            return
        route, value = asked[0]
        if len(names) == 2:
            value = jnp.where(self.end, value, asked[1][1])
        got = lax.ppermute(value, ("dp", "tensor"), self.route[route])
        self.last = (value,)
        for name in names:
            self.flows[name][1] = got

    def take(self, piece, which):
        rows = piece.shape[0] // 2
        return lax.dynamic_slice_in_dim(piece, which * rows, rows, 0)

    def join(self, half, other, which):
        return jnp.concatenate(
            [jnp.where(which == 0, half, other), jnp.where(which == 0, other, half)]
        )

    def opening(self, route, value):
        yield "sent", (yield route, self.hold(value))

    def line_sum(self, own, other, rows):
        own, other = self.hold((own, other))
        half = own[rows] + other[rows]
        half = half + (yield "near", half)
        half = half + (yield "middle", half)
        half = jnp.where(self.end, (yield "near", half), half)
        yield "done", (half, (yield "pair", half))

    def fold_sum(self, own, other, rows):
        own, other = self.hold((own, other))
        place = lax.axis_index("dp") >> 2
        half = own[rows] + other[rows]
        part = self.take(half, place)
        part = part + (yield "cross", self.take(half, 1 - place))
        part = part + (yield "pair", part)
        half = self.join(part, (yield "cross", part), place)
        yield "done", (half, (yield "near", half))

    def whole_sum(self, array):
        array = self.hold(array)
        half = self.take(array, self.side)
        half = half + (yield "pair", self.take(array, 1 - self.side))
        half = half + (yield "near", half)
        half = half + (yield "middle", half)
        half = jnp.where(self.end, (yield "near", half), half)
        yield "done", self.join(half, (yield "pair", half), self.side)

    def scatter(self, array, axis):
        array = self.hold(array)
        size = array.shape[axis] // 4

        def part(which):
            return lax.dynamic_slice_in_dim(array, which * size, size, axis)

        far = yield "flip", part(self.rank ^ 3)
        near = yield "flip", part(self.rank ^ 1)
        over = yield "over", part(self.rank ^ 2) + far
        yield "done", part(self.rank) + near + over

    def gather(self, array):
        array = self.hold(array)
        rows = array.shape[0]
        other = yield "over", array
        pair = jnp.concatenate([array, other])
        crossed = yield "flip", pair
        full = jnp.zeros((4 * rows,) + array.shape[1:], array.dtype)
        for flip, value in zip((0, 2, 1, 3), (array, other, crossed[:rows], crossed[rows:])):
            full = lax.dynamic_update_slice_in_dim(full, value, (self.rank ^ flip) * rows, 0)
        yield "done", full


def on_device(
    tokens,
    segment,
    norm_gain,
    gate_weight,
    value_weight,
    state_weight,
    step_weight,
    value_filter,
    value_offset,
    state_filter,
    state_offset,
    step_offset,
    decay_log,
    skip_gain,
    inner_gain,
    output_weight,
    cotangent,
):
    groups = lax.axis_size("tensor")
    rank = lax.axis_index("tensor")
    channels = inner_gain.shape[0]
    inner_all = channels * groups
    heads = step_offset.shape[0]
    _, width = tokens.shape
    wide_states = state_weight.shape[1]
    cols = width // groups
    start = rank * cols
    cuts = width // channels
    folds = channels // wide_states

    live = (segment >= 0).astype(F32)[:, None]
    aux, seg_rows, ends = side_columns(segment)
    normed, gate, values, states, raw, masked, branch_grad = front(
        aux,
        tokens,
        cotangent,
        norm_gain,
        gate_weight,
        value_weight,
        state_weight,
        step_weight.T,
        output_weight,
    )
    shared = (
        value_filter,
        value_offset,
        state_filter,
        state_offset,
        step_offset,
        decay_log,
        skip_gain,
    )
    scanned, sums, kept = scan_forward(
        ends, aux, seg_rows, values, states, raw, gate, branch_grad, *shared, inner_gain
    )
    sums = lax.psum(sums, "tensor") / inner_all
    inner_scale = lax.rsqrt(sums[0] + EPS)
    pull = (inner_scale**3 * sums[1])[:, None]
    inner_scale = inner_scale[:, None]

    branch = scanned * (gate * sigmoid(gate)) * inner_scale * inner_gain[None, :]
    branch = branch.astype(BF16)

    def scale_of(rows):
        wide = rows.astype(F32)
        return lax.rsqrt(jnp.mean(wide * wide, axis=1, keepdims=True) + EPS)

    env = {}

    def half_of(array, which):
        return lax.dynamic_slice_in_dim(array, which * (width // 2), width // 2, 1)

    def cut(key, product):
        def send(hold):
            env[key] = product(hold, 1 - bit[key])
            return env[key]

        def keep(hold):
            env[key + "k"] = product(hold, bit[key])
            return env[key + "k"]

        return send, keep

    def to_gate(hold):
        y, gate_in, bg = hold((scanned, gate, branch_grad))
        gate_sig = sigmoid(gate_in)
        silu_gate = gate_in * gate_sig
        gated = y * silu_gate
        gated_grad = inner_scale * (bg * inner_gain[None, :]) - gated * pull
        gate_low = gated_grad * y * (gate_sig + silu_gate * (1.0 - gate_sig))
        env["gate_low"] = gate_low.astype(BF16)
        env["scanned_grad"] = gated_grad * silu_gate
        env["inner_gain"] = jnp.sum(bg * gated * inner_scale, axis=0)

    def out_product(hold, which):
        return tn(branch, half_of(hold(masked), which))

    def gate_product(hold, which):
        if "gate_low" not in env:
            to_gate(hold)
        return tn(half_of(normed, which), hold(env["gate_low"]))

    def value_product(hold, which):
        return tn(half_of(normed, which), hold(env["low"][0]))

    def bwd(hold):
        results = scan_backward(
            ends, aux, seg_rows, values, states, raw, hold(env["scanned_grad"]), kept, *shared
        )
        values_low, upper, lower, steps_low, by_channel, by_state, by_head = results
        env["low"] = (values_low, steps_low, upper, lower)
        env["sums"] = (by_channel, by_state, by_head)
        return values_low

    def grad(hold):
        values_low, steps_low, upper, lower = hold(env["low"])
        normed_grad = (
            nt(env["gate_low"], gate_weight)
            + nt(steps_low, step_weight)
            + nt(upper, state_weight)
            + nt(lower, state_weight)
            + nt(values_low, value_weight)
        )
        env["R"] = normed_grad
        rows = hold(tokens)
        env["scale"] = scale_of(rows)
        unit = rows.astype(F32) * env["scale"]
        env["along"] = jnp.sum(normed_grad * unit * norm_gain[None, :], axis=1)
        env["gain"] = jnp.sum(normed_grad * unit, axis=0)
        return normed_grad, env["along"], env["gain"]

    def state(hold):
        upper, lower = hold(env["low"][2:])
        env["U"] = tn(normed, upper) + tn(normed, lower)
        return env["U"]

    def out(hold):
        env["P"] = nn(hold(branch), output_weight)
        return env["P"]

    def tot(hold):
        env["along"], env["gain"], env["maps"] = lax.psum(
            hold((env["along"], env["gain"], env["sums"][1])), "tensor"
        )
        return env["along"], env["gain"], env["maps"]

    def rows_of(*items):
        laid = []
        for item in items:
            laid.append(jnp.pad(item, ((0, -item.shape[0] % 8), (0, channels - item.shape[1]))))
        return laid

    def pack(hold, part):
        by_channel, _, by_head = env["sums"]
        skip_part = jnp.sum(by_channel[5].reshape(heads, -1), axis=1)
        size = part.shape[0] // folds
        blocks = [part[i * size :][:size] for i in range(folds)]
        small = rows_of(
            jnp.concatenate(blocks, axis=1),
            by_channel,
            env["inner_gain"][None, :],
            hold(env["maps"]),
            jnp.stack([by_head[0], by_head[1], skip_part]),
        )
        step_grad = tn(env["low"][1], normed)
        for item in (env["gain"][None, :], step_grad):
            small.extend(rows_of(*(item[:, i * channels :][:, :channels] for i in range(cuts))))
        env["heights"] = [item.shape[0] for item in small]
        room = -sum(env["heights"]) % 16
        env["E"] = jnp.concatenate(small + [jnp.zeros((room, channels), F32)])
        return env["E"]

    def unfold(total):
        blocks = total[: env["heights"][0]]
        return jnp.concatenate(
            [blocks[:, i * wide_states :][:, :wide_states] for i in range(folds)]
        )

    def mixed_of(summed):
        token_share = lax.dynamic_slice_in_dim(tokens, start, cols, 1).astype(F32)
        return (token_share + live * summed).astype(BF16)

    def tokens_of(share_grad):
        unit_share = lax.dynamic_slice_in_dim(tokens, start, cols, 1).astype(F32) * env["scale"]
        gain_share = lax.dynamic_slice_in_dim(norm_gain, start, cols, 0)
        cotangent_share = lax.dynamic_slice_in_dim(cotangent, start, cols, 1).astype(F32)
        return cotangent_share + env["scale"] * (
            share_grad * gain_share[None, :] - unit_share * (env["along"] / width)[:, None]
        )

    if lax.axis_size("dp") != 8 or groups != 4:
        def hold(value):
            return value

        to_gate(hold)
        for task in (bwd, grad, state, out, tot):
            task(hold)
        part = lax.psum_scatter(env["U"], "tensor", scatter_dimension=0, tiled=True)
        pack(hold, part)
        mixed = mixed_of(lax.psum_scatter(env["P"], "tensor", scatter_dimension=1, tiled=True))
        shared_grad = lax.psum_scatter(env["R"], "tensor", scatter_dimension=1, tiled=True)
        tokens_grad = tokens_of(shared_grad)
        output_grad, gate_weight_grad, value_weight_grad, small = lax.psum(
            (
                tn(branch, masked),
                tn(normed, env["gate_low"]),
                tn(normed, env["low"][0]),
                env["E"],
            ),
            "dp",
        )
        state_weight_grad = lax.all_gather(unfold(small), "tensor", axis=0, tiled=True)
    else:
        plan = Schedule()
        bit = {key: plan.side if KINDS[key][0] == "A" else plan.fold for key in "OGX"}
        so, ko = cut("O", out_product)
        sg, kg = cut("G", gate_product)
        sx, kx = cut("X", value_product)
        tasks = dict(so=so, ko=ko, sg=sg, kg=kg, sx=sx, kx=kx, bwd=bwd)
        tasks.update(grad=grad, state=state, out=out, tot=tot)
        tasks["pack"] = lambda hold: pack(hold, plan.done["U"])
        for entry in ORDER:
            if entry[0] == "*":
                result = tasks[entry[1:]](plan.hold)
                plan.last = result if isinstance(result, tuple) else (result,)
                continue
            names = entry.split("+")
            for name in names:
                if name in plan.flows:
                    continue
                if name in "PR":
                    flow = plan.scatter(env[name], 1)
                elif name == "U":
                    flow = plan.scatter(env[name], 0)
                elif name == "K":
                    flow = plan.gather(unfold(plan.done["E"]))
                elif name == "E":
                    flow = plan.whole_sum(env["E"])
                elif len(name) == 1:
                    flow = plan.opening("pair" if KINDS[name][0] == "A" else "near", env[name])
                else:
                    key, i = name[0], int(name[1:])
                    rows = env[key].shape[0] // int(KINDS[key][1:])
                    flow = plan.line_sum if KINDS[key][0] == "A" else plan.fold_sum
                    part = slice(i * rows, (i + 1) * rows)
                    flow = flow(env[key + "k"], plan.flows[key][1], part)
                plan.add(name, flow)
            plan.step(names)
        mixed = mixed_of(plan.done["P"])
        tokens_grad = tokens_of(plan.done["R"])
        state_weight_grad = plan.done["K"]
        totals = {}
        for key in "OGX":
            got = [plan.done[f"{key}{i}"] for i in range(int(KINDS[key][1:]))]
            low = [jnp.where(bit[key] == 0, half, other) for half, other in got]
            high = [jnp.where(bit[key] == 0, other, half) for half, other in got]
            if key == "O":
                sides = [jnp.concatenate([lo, hi], axis=1) for lo, hi in zip(low, high)]
                totals[key] = jnp.concatenate(sides)
            else:
                totals[key] = jnp.concatenate(low + high)
        output_grad, gate_weight_grad, value_weight_grad = (totals[key] for key in "OGX")
        small = plan.done["E"]
    parts = []
    for height in env["heights"]:
        parts.append(small[:height])
        small = small[height:]
    chan, inner_grad, state_pair, head = parts[1:5]
    gain_grad = jnp.concatenate([part[0] for part in parts[5 : 5 + cuts]])
    step_grad = jnp.concatenate([part[:heads] for part in parts[5 + cuts :]], axis=1)
    state_pair = state_pair[:, :wide_states]
    off, dec, skip = (head[i, :heads] for i in range(3))
    return (
        mixed,
        tokens_grad,
        gain_grad,
        gate_weight_grad,
        value_weight_grad,
        state_weight_grad,
        step_grad.T,
        chan[:4],
        chan[4],
        state_pair[:4],
        state_pair[4],
        off,
        dec,
        skip,
        inner_grad[0],
        output_grad,
    )


def solution(mesh):
    tokens = P("dp", None)
    columns = P(None, "tensor")
    split = P("tensor")

    return jax.shard_map(
        on_device,
        mesh=mesh,
        in_specs=(
            tokens,
            P("dp"),
            P(),
            columns,
            columns,
            P(),
            columns,
            columns,
            split,
            P(),
            P(),
            split,
            split,
            split,
            split,
            P("tensor", None),
            tokens,
        ),
        out_specs=(
            P("dp", "tensor"),
            P("dp", "tensor"),
            P(),
            columns,
            columns,
            P(),
            columns,
            columns,
            split,
            P(),
            P(),
            split,
            split,
            split,
            split,
            P("tensor", None),
        ),
        check_vma=False,
    )
```
